32 devices in a mesh: replica: 16 (over z, x, core), shard: 2 (over y).
Axes of the slice: x: 2, y: 2, z: 4, core: 2. Of those that a mesh axis runs over, the one named last changes fastest.
Arguments:
- frames: bfloat16 [32768, 768], P(('replica', 'shard')), may hold values from -6 to 6
- cotangent: bfloat16 [32768, 768], P(('replica', 'shard')), may hold values from -6 to 6
- segment_ids: int32 [32, 1024], P(('replica', 'shard')), may hold values from 0 to 7, never falling along the last dimension, each value on 1 to 512 neighbouring positions
- norm_gain: bfloat16 [2, 768], P(None, 'shard'), may hold values from 0.099609375 to 1.8984375
- norm_bias: bfloat16 [2, 768], P(None, 'shard'), may hold values from -2 to 2
- w_qkv: bfloat16 [768, 2304], P('shard'), may hold values from -0.21875 to 0.21875
- qv_bias: bfloat16 [2, 768], P(None, 'shard'), may hold values from -2 to 2
- w_out: bfloat16 [768, 768], P('shard'), may hold values from -0.875 to 0.875
- out_bias: bfloat16 [2, 768], P(None, 'shard'), may hold values from -2 to 2
- w_up: bfloat16 [768, 3072], P(None, 'shard'), may hold values from -0.21875 to 0.21875
- up_bias: bfloat16 [3072], P('shard'), may hold values from -3 to 3
- w_down: bfloat16 [3072, 768], P('shard'), may hold values from -0.109375 to 0.109375
Outputs:
- out_frames: bfloat16 [32768, 768], P(('replica', 'shard'))
- d_frames: float32 [32768, 768], P(('replica', 'shard'))
- d_norm_gain: float32 [2, 768], P(None, 'shard')
- d_norm_bias: float32 [2, 768], P(None, 'shard')
- d_w_qkv: float32 [768, 2304], P('shard')
- d_qv_bias: float32 [2, 768], P(None, 'shard')
- d_w_out: float32 [768, 768], P('shard')
- d_out_bias: float32 [2, 768], P(None, 'shard')
- d_w_up: float32 [768, 3072], P(None, 'shard')
- d_up_bias: float32 [3072], P('shard')
- d_w_down: float32 [3072, 768], P('shard')
The draws below stay inside these ranges and needn't reach their ends.
Inputs may be any that keep to these rules, and one draw needn't show every extreme that they name: `segment_ids`: each row numbers the documents of one sequence in order: never falling, every number of 0 to 7 used, no document longer than 512 frames, and one exactly that long in every row.
All inputs are finite; a program needn't handle non-finite values.
Results may differ from the reference program's by a relative error of at most 0.018.
Values may be sent and summed in bfloat16 or wider, within the bound.
No kernel may reach another device: no remote copies, remote signals or barrier semaphores. Data moves between devices by JAX's collectives and lax.ppermute only.
A program may use at most 256 MiB of HBM per device.

```python
import math
import jax
import jax.numpy as jnp
import numpy as np
from jax import lax

D = 768
H = 12
DH = 64
FF = 3072
LENGTH = 1024
DOCS = 8
SEQS = 32
TOKENS = 32768


def with_spikes(drawn, stream_key, source, target, shards_of, factor):
    def block_of(axis_at):
        return (jnp.arange(drawn.shape[axis_at]) // (drawn.shape[axis_at] // shards_of)).reshape((-1,) + (1,) * (drawn.ndim - 1 - axis_at))

    one_side = jax.random.permutation(stream_key, shards_of)[block_of(target)]
    other_side = (block_of(target) + shards_of // 2) % shards_of
    return jnp.where((block_of(source) == one_side) | (block_of(source) == other_side), factor * drawn, drawn)


def shard_levels(rng, dims, shards, smallest, high):
    loudness = 1.0
    for dim, parts in shards:
        heights = jax.random.uniform(jax.random.fold_in(jax.random.fold_in(rng, 6), dim), (parts,), jnp.float32, smallest / len(shards), high / len(shards))
        loudness = loudness * jnp.repeat(jnp.exp(heights), dims[dim] // parts).reshape((-1,) + (1,) * (len(dims) - 1 - dim))
    return loudness


def split_up(count, total, reach, slope):
    weights = [(1 << 20) // math.isqrt(grade ** slope) + 1 for grade in range(2, count + 1)]
    rest, holding = total - reach - (count - 1), [1] * (count - 1)
    while rest > 0:
        candidates = [i for i in range(count - 1) if holding[i] < reach]
        whole, remaining = sum([weights[i] for i in candidates]), rest
        for i in candidates:
            addition = min(reach - holding[i], max(1, remaining * weights[i] // whole), rest)
            holding[i] = holding[i] + addition
            rest = rest - addition
    return np.array([reach] + holding)


def uneven_parts(key, count, total, bound, slope):
    if count == 2:
        one = jax.random.randint(key, (), max(1, total - bound), min(bound, total - 1) + 1)
        return jnp.stack([one, total - one])
    tallies = jnp.asarray(split_up(count, total, bound, slope), jnp.int32)
    twos = (count - 1) // 2
    donor, receiver = tallies[1:1 + 2 * twos:2], tallies[2:2 + 2 * twos:2]
    slack = jnp.minimum(donor - 1, bound - receiver)
    passed = jax.random.randint(jax.random.fold_in(key, 1), (twos,), 0, 1 << 20) % (slack + 1)
    tallies = tallies.at[1:1 + 2 * twos:2].set(donor - passed).at[2:2 + 2 * twos:2].set(receiver + passed)
    return tallies[jax.random.permutation(jax.random.fold_in(key, 2), count)]


def centred(stream_key, shape, deviation, reach, cuts=(), held_as=jnp.bfloat16):
    gain = shard_levels(stream_key, shape, cuts, -0.22, 0.18) if cuts else 1.0
    values = jax.random.normal(stream_key, shape, jnp.float32) * deviation * gain
    return jnp.minimum(jnp.maximum(values, -reach), reach).astype(held_as)


def heavy_noise(key, shape, scale, reach, pieces, heavy, held_as=jnp.bfloat16):
    entries = scale * jax.random.normal(key, shape, jnp.float32)
    if pieces:
        entries = entries * shard_levels(key, shape, pieces, -0.22, 0.18)
    return jnp.clip(with_spikes(entries, jax.random.fold_in(key, 3), *heavy), -reach, reach).astype(held_as)


def setup_inputs(seed: int = 0) -> dict:
    key_list = jax.random.split(jax.random.key(seed), 13)
    return {
        "frames": centred(key_list[0], (TOKENS, D), 1.0, 6.0, ((0, 32),)),
        "cotangent": heavy_noise(key_list[1], (TOKENS, D), 1.0, 6.0, ((0, 32),), (0, 1, 32, 2.75)),
        "segment_ids": jax.vmap(lambda own: jnp.searchsorted(jnp.cumsum(uneven_parts(own, DOCS, LENGTH, LENGTH // 2, 3)), jnp.arange(LENGTH), side="right"))(jax.random.split(key_list[2], SEQS)).reshape((SEQS, LENGTH)).astype(jnp.int32),
        "norm_gain": jnp.clip(1.0 + 0.18 * jax.random.normal(key_list[3], (2, D), jnp.float32), 0.099609375, 1.8984375).astype(jnp.bfloat16),
        "norm_bias": centred(key_list[4], (2, D), 0.3, 2.0, ((1, 2),)),
        "w_qkv": centred(key_list[5], (D, 3 * D), D ** -0.5, 0.21875, ((0, 2),)),
        "qv_bias": centred(key_list[6], (2, D), 0.3, 2.0, ((1, 2),)),
        "w_out": centred(key_list[7], (D, D), (D // 16) ** -0.5, 0.875, ((0, 2),)),
        "out_bias": centred(key_list[8], (2, D), 0.3, 2.0, ((1, 2),)),
        "w_up": centred(key_list[9], (D, FF), D ** -0.5, 0.21875, ((1, 2),)),
        "up_bias": centred(key_list[10], (FF,), 0.5, 3.0, ((0, 2),)),
        "w_down": centred(key_list[11], (FF, D), FF ** -0.5, 0.109375, ((0, 2),)),
    }


EPS = 1e-05
NEG = -1e+30

@jax.custom_vjp
def low(v):
    return lax.optimization_barrier(v.astype(jnp.bfloat16)).astype(jnp.float32)

@jax.custom_vjp
def low_back(v):
    return v

def low_keep(v):
    return (low(v), None)

def low_pass(kept, grad):
    return (grad,)

def back_keep(v):
    return (v, None)

def back_low(kept, grad):
    return (low(grad),)
low.defvjp(low_keep, low_pass)
low_back.defvjp(back_keep, back_low)

def matmul(left, right):
    return jnp.dot(left, right, precision=lax.Precision.HIGHEST)

def standardize(values):
    centered = values - lax.optimization_barrier(jnp.mean(values, axis=-1, keepdims=True))
    return centered * lax.rsqrt(lax.optimization_barrier(jnp.mean(centered * centered, axis=-1, keepdims=True)) + EPS)

def attend(queries, key_rows, value_rows, segment):
    length = segment.shape[0]
    shaped = (length, H, DH)
    raw = jnp.einsum('qhd,khd->hqk', queries.reshape(shaped), key_rows.reshape(shaped), precision=lax.Precision.HIGHEST) * (1.0 / math.sqrt(DH))
    same = segment[:, None] == segment[None, :]
    scores = jnp.where(same[None], low_back(raw), NEG)
    probs = jax.nn.softmax(scores, axis=-1)
    mixed = jnp.einsum('hqk,khd->qhd', low(probs), value_rows.reshape(shaped), precision=lax.Precision.HIGHEST)
    return mixed.reshape(length, H * DH)

def forward(inputs, gains, shifts, qkv_weight, qv_shift, out_weight, out_shift, up_weight, up_shift, down_weight, segments):
    width = inputs.shape[1]
    count, length = segments.shape
    normed = low(standardize(inputs) * gains[0] + shifts[0])
    projected = matmul(normed, qkv_weight)
    queries = low_back(low(projected[:, :width] + qv_shift[0]))
    key_rows = low_back(low(projected[:, width:2 * width]))
    value_rows = low_back(low(projected[:, 2 * width:] + qv_shift[1]))
    mixed = jax.vmap(attend)(queries.reshape(count, length, width), key_rows.reshape(count, length, width), value_rows.reshape(count, length, width), segments)
    mixed = low_back(low(mixed.reshape(count * length, width)))
    middle = inputs + low_back(matmul(mixed, out_weight) + out_shift[0])
    normed_two = low(standardize(middle) * gains[1] + shifts[1])
    hidden = low_back(matmul(normed_two, up_weight) + up_shift)
    activated = low(jax.nn.gelu(hidden, approximate=False))
    return middle + low_back(matmul(activated, down_weight) + out_shift[1])

def reference(frames, cotangent, segment_ids, norm_gain, norm_bias, w_qkv, qv_bias, w_out, out_bias, w_up, up_bias, w_down):
    params = tuple((array.astype(jnp.float32) for array in (norm_gain, norm_bias, w_qkv, qv_bias, w_out, out_bias, w_up, up_bias, w_down)))
    seq_count = segment_ids.shape[0]
    group = math.gcd(4, seq_count)
    turns = seq_count // group
    width = frames.shape[1]
    inputs_all = frames.astype(jnp.float32).reshape(turns, group * LENGTH, width)
    grads_all = cotangent.astype(jnp.float32).reshape(turns, group * LENGTH, width)
    segs_all = segment_ids.reshape(turns, group, LENGTH)

    def one_group(running, batch_item):
        inputs, grad_out, segments = batch_item

        def local(*values):
            return forward(*values, segments)
        result, pull = jax.vjp(local, inputs, *params)
        gradients = pull(grad_out)
        running = tuple((summed + gradient for summed, gradient in zip(running, gradients[1:])))
        return (running, (result, gradients[0]))
    zeros = tuple((jnp.zeros_like(array) for array in params))
    sums, (results, grad_inputs) = lax.scan(one_group, zeros, (inputs_all, grads_all, segs_all))
    return (results.reshape(-1, width).astype(jnp.bfloat16), grad_inputs.reshape(-1, width), sums[0], sums[1], sums[2], sums[3], sums[4], sums[5], sums[6], sums[7], sums[8])
```

```python
import functools
import math

import jax
import jax.numpy as jnp
from jax import lax
from jax.experimental import pallas as pl
from jax.experimental.pallas import tpu as pltpu
from jax.sharding import PartitionSpec as P

H = 12
EPS = 1e-05
NEG = -1e30
F32 = jnp.float32
BF = jnp.bfloat16
NN = (((1,), (0,)), ((), ()))
NT = (((1,), (1,)), ((), ()))
TN = (((0,), (0,)), ((), ()))
BLK = 256
GROUPS = 3
VM = pl.BlockSpec(memory_space=pltpu.VMEM)
SM = pl.BlockSpec(memory_space=pltpu.SMEM)
LIMIT = 48 << 20


def mm(a, b, dims=NN):
    return lax.dot_general(a, b, dims, preferred_element_type=F32)


def rows_of(i, size=BLK):
    return pl.ds(pl.multiple_of(i * size, size), size)


def call(kernel, name, outs, n_in, smem, scratch=(), flops=0, moved=0, trans=0):
    return pl.pallas_call(
        kernel,
        name=name,
        out_shape=outs,
        in_specs=[SM] * smem + [VM] * (n_in - smem),
        out_specs=jax.tree.map(lambda _: VM, outs),
        scratch_shapes=list(scratch),
        compiler_params=pltpu.CompilerParams(vmem_limit_bytes=LIMIT),
        cost_estimate=pl.CostEstimate(flops=flops, bytes_accessed=moved, transcendentals=trans),
    )


def array(shape, dtype=BF):
    return jax.ShapeDtypeStruct(shape, dtype)


def standardize(values):
    centered = values - jnp.mean(values, axis=1, keepdims=True)
    inverse = lax.rsqrt(jnp.mean(centered * centered, axis=1, keepdims=True) + EPS)
    return centered * inverse, inverse


def enter_kernel(frames_ref, cot_ref, gain_ref, shift_ref, normed_ref, normedT_ref, sum_ref):
    sum_ref[...] = jnp.zeros_like(sum_ref)

    def step(i, _):
        at = rows_of(i)
        unit, _inv = standardize(frames_ref[at, :].astype(F32))
        normed = (unit * gain_ref[0:1, :] + shift_ref[0:1, :]).astype(BF)
        normed_ref[at, :] = normed
        normedT_ref[:, at] = normed.T
        sum_ref[...] += jnp.sum(cot_ref[at, :].astype(F32), axis=0, keepdims=True)
        return 0

    lax.fori_loop(0, frames_ref.shape[0] // BLK, step, 0)


def enter(frames, cot, gain, shift):
    rows, width = frames.shape
    return call(
        enter_kernel, "enter", (array((rows, width)), array((width, rows)), array((1, width), F32)), 4, 0,
        flops=rows * width * 20, moved=rows * width * 8,
    )(frames, cot, gain, shift)


def windows(seg):
    length = seg.shape[1]
    first = seg[0, ::BLK]
    last = seg[0, BLK - 1 :: BLK]
    begin = jnp.sum((seg < first[:, None]).astype(jnp.int32), axis=1)
    end = jnp.sum((seg <= last[:, None]).astype(jnp.int32), axis=1)
    begin = begin // 16 * 16
    count = (end - begin + BLK - 1) // BLK
    begin = jnp.minimum(begin, length - count * BLK)
    return jnp.stack([begin, count]).astype(jnp.int32)


def by_head(block, dh):
    width = block.shape[1]
    lane = lax.broadcasted_iota(jnp.int32, (1, width), 1) // dh
    zero = jnp.zeros_like(block)
    return jnp.concatenate([jnp.where(lane == h, block, zero) for h in range(width // dh)], axis=0)


def place(full_ref, pos_ref, own_ref, near_ref, far_ref):
    shard, core = pos_ref[0], pos_ref[1]
    size = own_ref.shape[0]
    half = size // 2
    full_ref[pl.ds(pl.multiple_of(shard * size, half), size), :] = own_ref[...]
    for k in range(near_ref.shape[0]):
        base = jnp.bitwise_xor(shard, k + 1) * size
        full_ref[pl.ds(pl.multiple_of(base + core * half, half), half), :] = near_ref[k]
        full_ref[pl.ds(pl.multiple_of(base + (1 - core) * half, half), half), :] = far_ref[k]


def attn_fwd_kernel(dh, pos_ref, win_ref, normed_ref, own_ref, near_ref, far_ref, bias_ref, segr_ref, segc_ref,
                    w_ref, proj_ref, att_ref, attT_ref, lse_ref, acc_ref):
    width = att_ref.shape[1]
    heads = width // dh
    length = normed_ref.shape[0]
    place(w_ref, pos_ref, own_ref, near_ref, far_ref)

    def project(i, _):
        at = rows_of(i)
        proj_ref[at, :] = (mm(normed_ref[at, :], w_ref[...]) + bias_ref[...]).astype(BF)
        return 0

    lax.fori_loop(0, length // BLK, project, 0)

    def queries(step, _):
        at = rows_of(step)
        q = (proj_ref[at, 0:width].astype(F32) * (1.0 / math.sqrt(dh))).astype(BF)
        qall = by_head(q, dh)
        segq = jnp.concatenate([segr_ref[:, at]] * heads, axis=1)
        acc_ref[...] = jnp.zeros_like(acc_ref)
        start = win_ref[0, step]

        def tile(j, carry):
            m_old, mass = carry
            ks = pl.ds(pl.multiple_of(start + j * BLK, 16), BLK)
            vT = proj_ref[ks, 2 * width : 3 * width].T
            same = segc_ref[ks, :] == segq
            s = jnp.where(same, mm(proj_ref[ks, width : 2 * width], qall, NT), NEG)
            m_new = jnp.maximum(m_old, jnp.max(s, axis=0, keepdims=True))
            p = jnp.exp(s - m_new)
            alpha = jnp.exp(m_old - m_new)
            mass = mass * alpha + jnp.sum(p, axis=0, keepdims=True)
            pb = p.astype(BF)
            for h in range(heads):
                hs, cs = slice(h * dh, (h + 1) * dh), slice(h * BLK, (h + 1) * BLK)
                acc_ref[hs, :] = acc_ref[hs, :] * alpha[:, cs] + mm(vT[hs, :], pb[:, cs])
            return m_new, mass

        carry = (jnp.full((1, heads * BLK), NEG, F32), jnp.zeros((1, heads * BLK), F32))
        peak, mass = lax.fori_loop(0, win_ref[1, step], tile, carry)
        lse_ref[:, rows_of(step, heads * BLK)] = peak + jnp.log(mass)
        outs = []
        for h in range(heads):
            outs.append((acc_ref[h * dh : (h + 1) * dh, :] / mass[:, h * BLK : (h + 1) * BLK]).astype(BF))
        oT = jnp.concatenate(outs, axis=0)
        attT_ref[:, at] = oT
        att_ref[at, :] = oT.T
        return 0

    lax.fori_loop(0, length // BLK, queries, 0)


def attn_fwd(dh, pos, win, normed, own, near, far, bias, segr, segc):
    length, d = normed.shape
    width = own.shape[1] // 3
    heads = width // dh
    return call(
        functools.partial(attn_fwd_kernel, dh), "attn_fwd",
        (array((d, 3 * width)), array((length, 3 * width)), array((length, width)), array((width, length)),
         array((1, length * heads), F32)),
        9, 2, [pltpu.VMEM((width, BLK), F32)],
        flops=2 * length * d * 3 * width + 2 * length * length * 256 * heads,
        trans=length * length * heads // 2, moved=length * (d + 6 * width) * 2,
    )(pos, win, normed, own, near, far, bias, segr, segc)


def attn_bwd_kernel(dh, pos_ref, win_ref, proj_ref, att_ref, g_ref, lse_ref, segr_ref, segc_ref, nT_ref,
                    dproj_ref, dw_ref, sums_ref, dk_ref, dv_ref, dqT_ref):
    length, width = att_ref.shape
    heads = width // dh
    scale = 1.0 / math.sqrt(dh)
    dk_ref[...] = jnp.zeros_like(dk_ref)
    dv_ref[...] = jnp.zeros_like(dv_ref)
    row = lax.broadcasted_iota(jnp.int32, (8, width), 0)
    col = lax.broadcasted_iota(jnp.int32, (8, width), 1) // dh
    pick = jnp.where(row == col, 1.0, 0.0).astype(BF)

    def queries(step, _):
        at = rows_of(step)
        q = (proj_ref[at, 0:width].astype(F32) * scale).astype(BF)
        g = g_ref[at, :]
        qall = by_head(q, dh)
        gall = by_head(g, dh)
        og = att_ref[at, :].astype(F32) * g.astype(F32)
        high = og.astype(BF)
        low = (og - high.astype(F32)).astype(BF)
        delta = mm(pick, high, NT) + mm(pick, low, NT)
        delta = jnp.concatenate([delta[h : h + 1, :] for h in range(heads)], axis=1)
        lse = lse_ref[:, rows_of(step, heads * BLK)]
        segq = jnp.concatenate([segr_ref[:, at]] * heads, axis=1)
        dqT_ref[...] = jnp.zeros_like(dqT_ref)
        start = win_ref[0, step]

        def tile(j, _):
            ks = pl.ds(pl.multiple_of(start + j * BLK, 16), BLK)
            kt = proj_ref[ks, width : 2 * width]
            vt = proj_ref[ks, 2 * width : 3 * width]
            kT = kt.T
            same = segc_ref[ks, :] == segq
            p = jnp.where(same, jnp.exp(mm(kt, qall, NT) - lse), 0.0)
            ds = (p * (mm(vt, gall, NT) - delta)).astype(BF)
            dv_ref[ks, :] += mm(p.astype(BF), gall)
            dk_ref[ks, :] += mm(ds, qall)
            for h in range(heads):
                hs = slice(h * dh, (h + 1) * dh)
                dqT_ref[hs, :] += mm(kT[hs, :], ds[:, h * BLK : (h + 1) * BLK])
            return 0

        lax.fori_loop(0, win_ref[1, step], tile, 0)
        dproj_ref[at, 0:width] = (dqT_ref[...] * scale).astype(BF).T
        return 0

    lax.fori_loop(0, length // BLK, queries, 0)
    dproj_ref[:, width : 2 * width] = dk_ref[...].astype(BF)
    dproj_ref[:, 2 * width :] = dv_ref[...].astype(BF)
    sums_ref[...] = jnp.sum(dproj_ref[...].astype(F32), axis=0, keepdims=True)
    piece = dw_ref.shape[1]
    for k in range(dw_ref.shape[0]):
        rs = pl.ds(pl.multiple_of(jnp.bitwise_xor(pos_ref[0], k) * piece, piece), piece)
        dw_ref[k] = mm(nT_ref[rs, :], dproj_ref[...]).astype(BF)


def attn_bwd(dh, pos, win, shards, proj, att, g, lse, segr, segc, nT):
    length, width = att.shape
    d = nT.shape[0]
    heads = width // dh
    return call(
        functools.partial(attn_bwd_kernel, dh), "attn_bwd",
        (array((length, 3 * width)), array((shards, d // shards, 3 * width)), array((1, 3 * width), F32)),
        9, 2, [pltpu.VMEM((length, width), F32), pltpu.VMEM((length, width), F32), pltpu.VMEM((width, BLK), F32)],
        flops=2 * length * d * 3 * width + 5 * length * length * 256 * heads,
        trans=length * length * heads // 2, moved=length * (d + 8 * width) * 2,
    )(pos, win, proj, att, g, lse, segr, segc, nT)


def middle_kernel(pos_ref, frames_ref, a0, a1, a2, own_ref, near_ref, far_ref, outb_ref, gain_ref, shift_ref,
                  w_ref, middle_ref, n_ref, nT_ref):
    place(w_ref, pos_ref, own_ref, near_ref, far_ref)
    width = a0.shape[1]

    def step(i, _):
        at = rows_of(i)
        total = frames_ref[at, :].astype(F32) + outb_ref[0:1, :]
        for g, a in enumerate((a0, a1, a2)):
            total = total + mm(a[at, :], w_ref[g * width : (g + 1) * width, :])
        middle_ref[at, :] = total
        unit, _inv = standardize(total)
        normed = (unit * gain_ref[1:2, :] + shift_ref[1:2, :]).astype(BF)
        n_ref[at, :] = normed
        nT_ref[:, at] = normed.T
        return 0

    lax.fori_loop(0, frames_ref.shape[0] // BLK, step, 0)


def middle(pos, frames, atts, own, near, far, outb, gain, shift):
    rows, d = frames.shape
    return call(
        middle_kernel, "middle",
        (array((d, d)), array((rows, d), F32), array((rows, d)), array((d, rows))), 11, 1,
        flops=2 * rows * d * d, moved=rows * d * 12,
    )(pos, frames, *atts, own, near, far, outb, gain, shift)


def ffn_kernel(own, apart, fresh, offset, step, pos_ref, n_ref, nT_ref, cot_ref, *refs):
    refs = list(refs)
    first, second = refs.pop(0), refs.pop(0)
    if apart:
        first, second = (first, second), (refs.pop(0), refs.pop(0))
    bias_ref = refs.pop(0)
    prev_ref = None if fresh else refs.pop(0)
    act_ref, keep_ref, send_ref, bsum_ref, gn_ref = refs[:5]
    core = pos_ref[1]
    if own:
        up_ref, down_ref = first, second
    else:
        down_ref, up_ref = refs[5], refs[6]
        for ref, t in ((up_ref, 0), (down_ref, 1)):
            size = ref.shape[0] // 2
            ref[pl.ds(pl.multiple_of(core * size, size), size), :] = first[t][...]
            ref[pl.ds(pl.multiple_of((1 - core) * size, size), size), :] = second[t][...]
    d = n_ref.shape[1]
    chunk = act_ref.shape[1]
    gn_ref[...] = jnp.zeros_like(gn_ref) if fresh else prev_ref[...]

    def body(j, _):
        cs = rows_of(j, step)
        ws = pl.ds(pl.multiple_of(offset + j * step, step), step)
        up = up_ref[:, ws]
        hidden = mm(n_ref[...], up) + bias_ref[:, cs]
        grad = mm(cot_ref[...], down_ref[ws, :], NT)
        phi = 0.5 + 0.5 * lax.erf(hidden * (1.0 / math.sqrt(2.0)))
        bell = jnp.exp(hidden * hidden * -0.5) * (1.0 / math.sqrt(2.0 * math.pi))
        act = (hidden * phi).astype(BF)
        gh = (grad * (phi + hidden * bell)).astype(BF)
        act_ref[:, cs] = act
        bsum_ref[:, cs] = jnp.sum(gh.astype(F32), axis=0, keepdims=True)
        gn_ref[...] += mm(gh, up, NT)
        d_down = mm(act, cot_ref[...], TN).astype(BF)
        d_up = mm(nT_ref[...], gh).astype(BF)

        def store(down_to, up_to):
            down_to[cs, :] = d_down
            for r in range(d // chunk):
                at = pl.ds(pl.multiple_of(r * chunk + j * step, step), step)
                up_to[:, at] = d_up[r * chunk : (r + 1) * chunk, :]

        @pl.when(core == 0)
        def _():
            store(keep_ref, send_ref)

        @pl.when(core == 1)
        def _():
            store(send_ref, keep_ref)

        return 0

    lax.fori_loop(0, chunk // step, body, 0)


def ffn(own, offset, pos, n, nT, cot, first, second, bias, grad):
    rows, d = n.shape
    chunk = bias.shape[1]
    step = 256 if chunk % 256 == 0 else 128
    fresh = grad is None
    apart = isinstance(first, tuple)
    args = [pos, n, nT, cot, *(first + second if apart else (first, second)), bias] + ([] if fresh else [grad])
    outs = (array((rows, chunk)), array((chunk, d)), array((chunk, d)), array((1, chunk), F32), array((rows, d), F32))
    if not own:
        outs = outs + (array((chunk, d)),)
    return call(
        functools.partial(ffn_kernel, own, apart, fresh, offset, step), "ffn", outs,
        len(args), 1, [] if own else [pltpu.VMEM((d, chunk), BF)], flops=10 * rows * d * chunk,
        trans=3 * rows * chunk, moved=rows * d * 20,
    )(*args)


def turn_kernel(pos_ref, gn_ref, middle_ref, cot_ref, gain_ref, w_ref, t0, t1, t2,
                gm_ref, g0, g1, g2, dw_ref, sums_ref, branch_ref, mixT_ref):
    width = g0.shape[1]
    sums_ref[...] = jnp.zeros_like(sums_ref)
    for g, t in enumerate((t0, t1, t2)):
        mixT_ref[g * width : (g + 1) * width, :] = t[...]

    def step(i, _):
        at = rows_of(i)
        gn = gn_ref[at, :]
        unit, inverse = standardize(middle_ref[at, :])
        e = gn * gain_ref[1:2, :]
        gm = cot_ref[at, :].astype(F32) + inverse * (
            e - jnp.mean(e, axis=1, keepdims=True) - unit * jnp.mean(e * unit, axis=1, keepdims=True)
        )
        gm_ref[at, :] = gm
        branch = gm.astype(BF)
        branch_ref[at, :] = branch
        sums_ref[0:1, :] += jnp.sum(gn * unit, axis=0, keepdims=True)
        sums_ref[1:2, :] += jnp.sum(gn, axis=0, keepdims=True)
        sums_ref[2:3, :] += jnp.sum(branch.astype(F32), axis=0, keepdims=True)
        for g, out in enumerate((g0, g1, g2)):
            out[at, :] = mm(branch, w_ref[g * width : (g + 1) * width, :], NT).astype(BF)
        return 0

    lax.fori_loop(0, gn_ref.shape[0] // BLK, step, 0)
    piece = dw_ref.shape[1]
    for k in range(dw_ref.shape[0]):
        rs = pl.ds(pl.multiple_of(jnp.bitwise_xor(pos_ref[0], k) * piece, piece), piece)
        dw_ref[k] = mm(mixT_ref[rs, :], branch_ref[...]).astype(BF)


def turn(pos, shards, gn, mid, cot, gain, w, attTs):
    rows, d = gn.shape
    width = d // GROUPS
    return call(
        turn_kernel, "turn",
        (array((rows, d), F32),) + (array((rows, width)),) * 3 + (array((shards, d // shards, d)), array((8, d), F32)),
        9, 1, [pltpu.VMEM((rows, d), BF), pltpu.VMEM((d, rows), BF)],
        flops=4 * rows * d * d, moved=rows * d * 20,
    )(pos, gn, mid, cot, gain, w, *attTs)


def leave_kernel(frames_ref, gm_ref, gain_ref, p0, p1, p2, w0, w1, w2, out_ref, sums_ref):
    sums_ref[...] = jnp.zeros_like(sums_ref)

    def step(i, _):
        at = rows_of(i)
        gn = mm(p0[at, :], w0[...], NT) + mm(p1[at, :], w1[...], NT) + mm(p2[at, :], w2[...], NT)
        unit, inverse = standardize(frames_ref[at, :].astype(F32))
        e = gn * gain_ref[0:1, :]
        out_ref[at, :] = gm_ref[at, :] + inverse * (
            e - jnp.mean(e, axis=1, keepdims=True) - unit * jnp.mean(e * unit, axis=1, keepdims=True)
        )
        sums_ref[0:1, :] += jnp.sum(gn * unit, axis=0, keepdims=True)
        sums_ref[1:2, :] += jnp.sum(gn, axis=0, keepdims=True)
        return 0

    lax.fori_loop(0, frames_ref.shape[0] // BLK, step, 0)


def leave(frames, gm, gain, dprojs, ws):
    rows, d = frames.shape
    return call(
        leave_kernel, "leave", (array((rows, d), F32), array((8, d), F32)), 9, 0,
        flops=6 * rows * d * d, moved=rows * d * 16,
    )(frames, gm, gain, *dprojs, *ws)


def result_kernel(n, offsets, middle_ref, outb_ref, *refs):
    acts, downs, out_ref = refs[:n], refs[n : 2 * n], refs[2 * n]

    def step(i, _):
        at = rows_of(i)
        total = middle_ref[at, :] + outb_ref[1:2, :]
        for a, w, offset in zip(acts, downs, offsets):
            total = total + mm(a[at, :], w[offset : offset + a.shape[1], :])
        out_ref[at, :] = total.astype(BF)
        return 0

    lax.fori_loop(0, middle_ref.shape[0] // BLK, step, 0)


def result(mid, outb, acts, downs, offsets):
    rows, d = mid.shape
    n = len(acts)
    return call(
        functools.partial(result_kernel, n, offsets), "result", array((rows, d)), 2 + 2 * n, 0,
        flops=2 * rows * d * n * acts[0].shape[1], moved=rows * d * 14,
    )(mid, outb, *acts, *downs)


def swap(value, axis, size, bit):
    return lax.ppermute(value, axis, [(i, i ^ bit) for i in range(size)])


def after(value, *others):
    return lax.optimization_barrier((value, *others))[0]


def add(a, b):
    return (a.astype(F32) + b.astype(F32)).astype(a.dtype)


def bits_of(size):
    return [1 << b for b in range(size.bit_length() - 1)]


def spread(own, shards):
    stack = own[None]
    for bit in bits_of(shards):
        stack = jnp.concatenate([stack, swap(stack, "shard", shards, bit)], axis=0)
    return stack


def fetch(half, shards, replicas):
    if shards == 2:
        near = swap(half, "shard", 2, 1)[None]
    else:
        near = spread(half, shards)[1:]
    return near, swap(near, "replica", replicas, 1)


def reduce_shard(pieces, shards):
    for bit in reversed(bits_of(shards)):
        got = swap(jnp.stack(pieces[bit:]) if bit > 1 else pieces[1], "shard", shards, bit)
        pieces = [add(p, got[k] if bit > 1 else got) for k, p in enumerate(pieces[:bit])]
    return pieces[0]


def reduce_replica(total, replicas, which):
    bits = bits_of(replicas)[1:]
    rows = total.shape[0] // 2
    flag = (lax.axis_index("replica") // 2) % 2
    keep = lax.dynamic_slice_in_dim(total, flag * rows, rows, 0)
    send = lax.dynamic_slice_in_dim(total, (1 - flag) * rows, rows, 0)
    part = add(keep, swap(send, "replica", replicas, bits[0]))
    for bit in bits[1:]:
        part = add(part, swap(part, "replica", replicas, bit))
    other = swap(part, "replica", replicas, bits[0])
    full = jnp.where(flag == 0, jnp.concatenate([part, other]), jnp.concatenate([other, part]))
    twin = swap(full, "replica", replicas, 1)
    first = which == 0
    return jnp.where(first, full, twin), jnp.where(first, twin, full)


def natural(stack, shard, axis):
    shards = stack.shape[0]
    shape = list(stack.shape[1:])
    size = shape[axis]
    shape[axis] = size * shards
    out = jnp.zeros(shape, stack.dtype)
    for k in range(shards):
        at = [0] * len(shape)
        at[axis] = (shard ^ k) * size
        out = lax.dynamic_update_slice(out, stack[k], at)
    return out


def pieces_of(value, shards, shard, axis):
    size = value.shape[axis] // shards
    return [lax.dynamic_slice_in_dim(value, (shard ^ k) * size, size, axis) for k in range(shards)]


def local(replicas, shards, frames, cotangent, segment_ids, norm_gain, norm_bias, w_qkv, qv_bias, w_out, out_bias,
          w_up, up_bias, w_down):
    rows, d = frames.shape
    dh = d // H
    group = d // GROUPS
    piece = d // shards
    hid = up_bias.shape[0]
    chunks = max(1, hid // d)
    chunk = hid // chunks
    shard = lax.axis_index("shard")
    replica = lax.axis_index("replica")
    core = replica % 2
    pos = jnp.stack([shard, core]).astype(jnp.int32)

    small = jnp.concatenate([norm_gain, norm_bias, qv_bias, out_bias, up_bias.reshape(-1, piece)], axis=0)
    smalls = spread(small, shards)
    whole = natural(smalls[:, :8], shard, 1).astype(F32)
    gain, shift, qv, outb = whole[0:2], whole[2:4], whole[4:6], whole[6:8]
    up_bias_all = smalls[:, 8:].reshape(shards, 1, hid).astype(F32)

    half = piece // 2
    mine = lax.dynamic_slice_in_dim(w_qkv, core * half, half, 0).reshape(half, 3, GROUPS, group)
    own_qkv = w_qkv.reshape(piece, 3, GROUPS, group)
    qkv_halves = [mine[:, :, g].reshape(half, 3 * group) for g in range(GROUPS)]
    qkv_own = [own_qkv[:, :, g].reshape(piece, 3 * group) for g in range(GROUPS)]
    out_half = lax.dynamic_slice_in_dim(w_out, core * half, half, 0)
    up_half = lax.dynamic_slice_in_dim(w_up, core * (d // 2), d // 2, 0)
    down_half = lax.dynamic_slice_in_dim(w_down.reshape(chunks, 2, chunk // 2, d), core, 1, 1)
    fetched = []
    sends = list(qkv_halves) + [out_half]
    for i in range(chunks):
        up_part = up_half[:, i * chunk : (i + 1) * chunk]
        if chunk == d:
            sends.append(jnp.stack([up_part, down_half[i, 0]]))
        else:
            sends.append((up_part, down_half[i, 0]))
    for i, send in enumerate(sends):
        if i:
            send = after(send, fetched[max(0, i - 2)][0])
        if isinstance(send, tuple):
            a, b = [fetch(v, shards, replicas) for v in send]
            fetched.append(((a[0], b[0]), (a[1], b[1])))
        else:
            fetched.append(fetch(send, shards, replicas))

    win = windows(segment_ids)
    segc = segment_ids.reshape(rows, 1)
    normed, normedT, cot_sum = enter(frames, cotangent, gain, shift)
    zero = jnp.zeros((1, group), F32)
    ws, projs, atts, attTs, lses = [], [], [], [], []
    for g in range(GROUPS):
        cols = slice(g * group, (g + 1) * group)
        bias = jnp.concatenate([qv[0:1, cols], zero, qv[1:2, cols]], axis=1)
        w, proj, att, attT, lse = attn_fwd(dh, pos, win, normed, qkv_own[g], *fetched[g], bias, segment_ids, segc)
        ws.append(w)
        projs.append(proj)
        atts.append(att)
        attTs.append(attT)
        lses.append(lse)
    w_out_all, mid, n_two, nT_two = middle(pos, frames, atts, w_out, *fetched[GROUPS], outb, gain, shift)

    grad, acts, downs, offsets = None, [], [], []
    keeps = [[None] * chunks for _ in range(shards)]
    got = [[None] * chunks for _ in range(shards)]
    up_sums = [[None] * chunks for _ in range(shards)]
    for k in range(shards):
        for i in range(chunks):
            bias = up_bias_all[k, :, i * chunk : (i + 1) * chunk]
            if k == 0:
                out = ffn(True, i * chunk, pos, n_two, nT_two, cotangent, w_up, w_down, bias, grad)
                downs.append(w_down)
                offsets.append(i * chunk)
            else:
                near, far = fetched[GROUPS + 1 + i]
                if isinstance(near, tuple):
                    near = near[0][k - 1], near[1][k - 1]
                    far = far[0][k - 1], far[1][k - 1]
                    out = ffn(False, 0, pos, n_two, nT_two, cotangent, near, far, bias, grad)
                else:
                    out = ffn(False, 0, pos, n_two, nT_two, cotangent, near[k - 1], far[k - 1], bias, grad)
                downs.append(out[5])
                offsets.append(0)
            acts.append(out[0])
            keeps[k][i] = out[1]
            got[k][i] = swap(out[2], "replica", replicas, 1)
            up_sums[k][i] = out[3]
            grad = out[4]
    ffn_grads = []
    for i in range(chunks):
        sums = [add(keeps[k][i], got[k][i]) for k in range(shards)]
        ffn_grads.append(reduce_replica(reduce_shard(sums, shards), replicas, core))

    out = turn(pos, shards, grad, mid, cotangent, gain, w_out_all, attTs)
    gm, gs, d_out, sums_two = out[0], out[1:4], out[4], out[5]
    dprojs, dws, qv_sums = [], [], []
    for g in range(GROUPS):
        dproj, dw, sums = attn_bwd(dh, pos, win, shards, projs[g], atts[g], gs[g], lses[g], segment_ids, segc, normedT)
        dprojs.append(dproj)
        dws.append(dw)
        qv_sums.append(sums)
    d_frames, sums_one = leave(frames, gm, gain, dprojs, ws)
    attn_grads = []
    for a, b in ((d_out, dws[0]), (dws[1], dws[2])):
        keep = jnp.where(core == 0, a, b)
        send = jnp.where(core == 0, b, a)
        both = add(keep, swap(send, "replica", replicas, 1))
        attn_grads.append(reduce_replica(reduce_shard([both[k] for k in range(shards)], shards), replicas, core))

    qv_sum = jnp.concatenate(qv_sums, axis=0)
    tall = jnp.concatenate(
        [sums_one[0:1], sums_two[0:1], sums_one[1:2], sums_two[1:2], qv_sum[:, :group].reshape(1, d),
         qv_sum[:, 2 * group :].reshape(1, d), sums_two[2:3], cot_sum], axis=0)
    parts = pieces_of(tall, shards, shard, 1)
    parts = [jnp.concatenate([p.reshape(-1), *[u.reshape(-1) for u in up_sums[k]]]).reshape(-1, piece) for k, p in enumerate(parts)]
    vec = reduce_shard(parts, shards)
    for bit in bits_of(replicas):
        vec = add(vec, swap(vec, "replica", replicas, bit))

    out_frames = result(mid, outb, acts, downs, tuple(offsets))

    d_down = jnp.concatenate([c[0] for c in ffn_grads], axis=0).astype(F32)
    ups = []
    for c in ffn_grads:
        up = c[1]
        ups.append(jnp.concatenate([up[:, r * chunk : (r + 1) * chunk] for r in range(d // chunk)], axis=0))
    d_up = jnp.concatenate(ups, axis=1).astype(F32)
    d_wout = attn_grads[0][0].astype(F32)
    groups = [attn_grads[0][1], attn_grads[1][0], attn_grads[1][1]]
    d_qkv = jnp.concatenate([g[:, t * group : (t + 1) * group] for t in range(3) for g in groups], axis=1).astype(F32)
    return (
        out_frames, d_frames, vec[0:2], vec[2:4], d_qkv, vec[4:6], d_wout, vec[6:8], d_up,
        vec[8:].reshape(hid), d_down,
    )


def solution(mesh):
    both = P(("replica", "shard"), None)
    wide, tall, flat = P(None, "shard"), P("shard", None), P("shard")
    return jax.shard_map(
        functools.partial(local, mesh.shape["replica"], mesh.shape["shard"]),
        mesh=mesh,
        in_specs=(both, both, both, wide, wide, tall, wide, tall, wide, wide, flat, tall),
        out_specs=(both, both, wide, wide, tall, wide, tall, wide, wide, flat, tall),
        check_vma=False,
    )
```

```python
import functools
import math

import jax
import jax.numpy as jnp
from jax import lax
from jax.experimental import pallas as pl
from jax.experimental.pallas import tpu as pltpu
from jax.sharding import PartitionSpec as P

H = 12
EPS = 1e-05
NEG = -1e30
F32 = jnp.float32
BF = jnp.bfloat16
NN = (((1,), (0,)), ((), ()))
NT = (((1,), (1,)), ((), ()))
TN = (((0,), (0,)), ((), ()))
BLK = 256
GROUPS = 3
VM = pl.BlockSpec(memory_space=pltpu.VMEM)
SM = pl.BlockSpec(memory_space=pltpu.SMEM)
LIMIT = 14 << 20
ROWS = 512


def mm(a, b, dims=NN):
    return lax.dot_general(a, b, dims, preferred_element_type=F32)


def blocks(rows, body):
    for i in range(rows // ROWS):
        body(slice(i * ROWS, (i + 1) * ROWS))


def rows_of(i, size=BLK):
    return pl.ds(pl.multiple_of(i * size, size), size)


def call(kernel, name, outs, n_in, smem, scratch=(), flops=0, moved=0, far=(), fetch=(), limit=LIMIT, cost=4.0):
    outs = outs if isinstance(outs, tuple) else (outs,)
    fetch = dict(fetch)
    n_out = len(outs)
    scratch = list(scratch)
    n_scratch = len(scratch)
    manual = [outs[i] for i in far] + list(fetch.values())

    def body(*refs):
        ins, rest = list(refs[:n_in]), list(refs[n_in:])
        targets, rest = rest[:n_out], rest[n_out:]
        own, rest = rest[:n_scratch], rest[n_scratch:]
        sem, buffers = rest[-1], rest[:-1]
        reads, writes = {}, {}
        for j, i in enumerate(fetch):
            buffer = buffers[len(far) + j]
            reads[i] = pltpu.make_async_copy(ins[i], buffer, sem.at[len(far) + j])
            reads[i].start()
            ins[i] = buffer
        local_outs = list(targets)
        for j, i in enumerate(far):
            local_outs[i] = buffers[j]

        def done(i):
            writes[i] = pltpu.make_async_copy(buffers[far.index(i)], targets[i], sem.at[far.index(i)])
            writes[i].start()

        def need(i):
            if i in reads:
                reads.pop(i).wait()

        kernel(done, need, *ins, *local_outs, *own)
        for i in far:
            if i not in writes:
                done(i)
        for i in list(reads):
            need(i)
        for copy in writes.values():
            copy.wait()

    hbm = pl.BlockSpec(memory_space=pltpu.HBM)
    out = pl.pallas_call(
        body if manual else functools.partial(kernel, None, None),
        name=name,
        out_shape=tuple(pltpu.HBM(o.shape, o.dtype) if i in far else o for i, o in enumerate(outs)),
        in_specs=[hbm if i in fetch else SM if i < smem else VM for i in range(n_in)],
        out_specs=tuple(hbm if i in far else VM for i in range(n_out)),
        scratch_shapes=scratch + ([pltpu.VMEM(m.shape, m.dtype) for m in manual] + [pltpu.SemaphoreType.DMA((len(manual),))] if manual else []),
        compiler_params=pltpu.CompilerParams(vmem_limit_bytes=limit),
        cost_estimate=pl.CostEstimate(flops=int(flops * cost), bytes_accessed=int(moved * cost), transcendentals=0),
    )
    return out


def array(shape, dtype=BF):
    return jax.ShapeDtypeStruct(shape, dtype)


def standardize(values):
    centered = values - jnp.mean(values, axis=1, keepdims=True)
    inverse = lax.rsqrt(jnp.mean(centered * centered, axis=1, keepdims=True) + EPS)
    return centered * inverse, inverse


def enter_kernel(group, done, need, pos_ref, frames_ref, cot_ref, small_ref, far_ref, normed_ref, normedT_ref, sum_ref, whole_ref, *bias_refs):
    shard = pos_ref[0]
    size = small_ref.shape[1]
    shards = far_ref.shape[0] + 1
    for j in range(shards):
        value = jnp.where(shard == j, small_ref[...].astype(F32), 0.0)
        for k in range(1, shards):
            value = jnp.where(jnp.bitwise_xor(shard, k) == j, far_ref[k - 1].astype(F32), value)
        whole_ref[:, j * size : (j + 1) * size] = value
    for g, ref in enumerate(bias_refs):
        cols = slice(g * group, (g + 1) * group)
        ref[:, 0:group] = whole_ref[4:5, cols]
        ref[:, group : 2 * group] = jnp.zeros((1, group), F32)
        ref[:, 2 * group : 3 * group] = whole_ref[5:6, cols]
    sum_ref[...] = jnp.zeros_like(sum_ref)

    def step(at):
        unit, _inv = standardize(frames_ref[at, :].astype(F32))
        normed = (unit * whole_ref[0:1, :] + whole_ref[2:3, :]).astype(BF)
        normed_ref[at, :] = normed
        normedT_ref[:, at] = normed.T
        sum_ref[...] += jnp.sum(cot_ref[at, :].astype(F32), axis=0, keepdims=True)

    blocks(frames_ref.shape[0], step)


def enter(pos, frames, cot, small, far):
    rows, width = frames.shape
    group = width // GROUPS
    outs = (array((rows, width)), array((width, rows)), array((1, width), F32), array((8, width), F32))
    return call(
        functools.partial(enter_kernel, group), "enter", outs + (array((1, 3 * group), F32),) * GROUPS, 5, 1,
        flops=rows * width * 20, moved=rows * width * 8, far=(1,),
    )(pos, frames, cot, small, far)


def pack_kernel(group, done, need, pos_ref, w_ref, *outs):
    half = w_ref.shape[0] // 2
    d = group * GROUPS
    at = pl.ds(pl.multiple_of(pos_ref[1] * half, half), half)
    for g in range(GROUPS):
        for t in range(3):
            cols = slice(t * d + g * group, t * d + (g + 1) * group)
            to = slice(t * group, (t + 1) * group)
            outs[g][:, to] = w_ref[at, cols]
            outs[GROUPS + g][:, to] = w_ref[:, cols]


def pack(pos, w):
    rows, cols = w.shape
    group = cols // 3 // GROUPS
    return call(
        functools.partial(pack_kernel, group), "pack",
        (array((rows // 2, 3 * group)),) * GROUPS + (array((rows, 3 * group)),) * GROUPS, 2, 1, moved=rows * cols * 5,
    )(pos, w)


def pack_more_kernel(done, need, pos_ref, out_ref, up_ref, down_ref, half_ref, *outs):
    core = pos_ref[1]
    half = half_ref.shape[0]
    half_ref[...] = out_ref[pl.ds(pl.multiple_of(core * half, half), half), :]
    chunks = len(outs) // 2
    up_rows, down_rows = up_ref.shape[0] // 2, down_ref.shape[0] // chunks // 2
    chunk = 2 * down_rows
    for i in range(chunks):
        at = pl.ds(pl.multiple_of(core * up_rows, up_rows), up_rows)
        outs[2 * i][...] = up_ref[at, i * chunk : (i + 1) * chunk]
        at = pl.ds(pl.multiple_of(i * chunk + core * down_rows, down_rows), down_rows)
        outs[2 * i + 1][...] = down_ref[at, :]


def pack_more(pos, w_out, w_up, w_down, chunks):
    d, hid = w_up.shape
    chunk = hid // chunks
    return call(
        pack_more_kernel, "pack_more",
        (array((w_out.shape[0] // 2, d)),) + (array((d // 2, chunk)), array((chunk // 2, d))) * chunks, 4, 1,
        moved=d * hid * 6,
    )(pos, w_out, w_up, w_down)


def windows(seg):
    length = seg.shape[1]
    first = seg[0, ::BLK]
    last = seg[0, BLK - 1 :: BLK]
    begin = jnp.sum((seg < first[:, None]).astype(jnp.int32), axis=1)
    end = jnp.sum((seg <= last[:, None]).astype(jnp.int32), axis=1)
    begin = begin // 16 * 16
    count = (end - begin + BLK - 1) // BLK
    begin = jnp.minimum(begin, length - count * BLK)
    return jnp.stack([begin, count]).astype(jnp.int32)


def by_head(block, dh):
    width = block.shape[1]
    lane = lax.broadcasted_iota(jnp.int32, (1, width), 1) // dh
    zero = jnp.zeros_like(block)
    return jnp.concatenate([jnp.where(lane == h, block, zero) for h in range(width // dh)], axis=0)


def place(full_ref, pos_ref, own_ref, near_ref, far_ref):
    shard, core = pos_ref[0], pos_ref[1]
    size = own_ref.shape[0]
    half = size // 2
    full_ref[pl.ds(pl.multiple_of(shard * size, half), size), :] = own_ref[...]
    for k in range(near_ref.shape[0]):
        base = jnp.bitwise_xor(shard, k + 1) * size
        full_ref[pl.ds(pl.multiple_of(base + core * half, half), half), :] = near_ref[k]
        full_ref[pl.ds(pl.multiple_of(base + (1 - core) * half, half), half), :] = far_ref[k]


def attn_fwd_kernel(dh, done, need, pos_ref, win_ref, normed_ref, own_ref, near_ref, far_ref, bias_ref, segr_ref, segc_ref,
                    w_ref, proj_ref, att_ref, attT_ref, lse_ref, acc_ref):
    width = att_ref.shape[1]
    heads = width // dh
    length = normed_ref.shape[0]
    place(w_ref, pos_ref, own_ref, near_ref, far_ref)

    def project(i, _):
        at = rows_of(i)
        proj_ref[at, :] = (mm(normed_ref[at, :], w_ref[...]) + bias_ref[...]).astype(BF)
        return 0

    lax.fori_loop(0, length // BLK, project, 0)
    done(0)
    done(1)

    def queries(step, _):
        at = rows_of(step)
        q = (proj_ref[at, 0:width].astype(F32) * (1.0 / math.sqrt(dh))).astype(BF)
        qall = by_head(q, dh)
        segq = jnp.concatenate([segr_ref[:, at]] * heads, axis=1)
        acc_ref[...] = jnp.zeros_like(acc_ref)
        start = win_ref[0, step]

        def tile(j, carry):
            m_old, mass = carry
            ks = pl.ds(pl.multiple_of(start + j * BLK, 16), BLK)
            vT = proj_ref[ks, 2 * width : 3 * width].T
            same = segc_ref[ks, :] == segq
            s = jnp.where(same, mm(proj_ref[ks, width : 2 * width], qall, NT), NEG)
            m_new = jnp.maximum(m_old, jnp.max(s, axis=0, keepdims=True))
            p = jnp.exp(s - m_new)
            alpha = jnp.exp(m_old - m_new)
            mass = mass * alpha + jnp.sum(p, axis=0, keepdims=True)
            pb = p.astype(BF)
            for h in range(heads):
                hs, cs = slice(h * dh, (h + 1) * dh), slice(h * BLK, (h + 1) * BLK)
                acc_ref[hs, :] = acc_ref[hs, :] * alpha[:, cs] + mm(vT[hs, :], pb[:, cs])
            return m_new, mass

        carry = (jnp.full((1, heads * BLK), NEG, F32), jnp.zeros((1, heads * BLK), F32))
        peak, mass = lax.fori_loop(0, win_ref[1, step], tile, carry)
        lse_ref[:, rows_of(step, heads * BLK)] = peak + jnp.log(mass)
        outs = []
        for h in range(heads):
            outs.append((acc_ref[h * dh : (h + 1) * dh, :] / mass[:, h * BLK : (h + 1) * BLK]).astype(BF))
        oT = jnp.concatenate(outs, axis=0)
        attT_ref[:, at] = oT
        att_ref[at, :] = oT.T
        return 0

    lax.fori_loop(0, length // BLK, queries, 0)


def attn_fwd(dh, pos, win, normed, own, near, far, bias, segr, segc):
    length, d = normed.shape
    width = own.shape[1] // 3
    heads = width // dh
    return call(
        functools.partial(attn_fwd_kernel, dh), "attn_fwd",
        (array((d, 3 * width)), array((length, 3 * width)), array((length, width)), array((width, length)),
         array((1, length * heads), F32)),
        9, 2, [pltpu.VMEM((width, BLK), F32)],
        flops=2 * length * d * 3 * width + 2 * length * length * 256 * heads,
        moved=length * (d + 6 * width) * 2, far=(0, 1, 3), cost=0.1,
    )(pos, win, normed, own, near, far, bias, segr, segc)


def split_rows(pos_ref, left_ref, right, keep_ref, send_ref, first):
    shard, core = pos_ref[0], pos_ref[1]
    half = left_ref.shape[0] // keep_ref.shape[0] // 2
    for k in range(keep_ref.shape[0]):
        base = jnp.bitwise_xor(shard, k) * (2 * half)
        for ref, part in ((keep_ref, core), (send_ref, 1 - core)):
            rs = pl.ds(pl.multiple_of(base + part * half, half), half)
            ref[k, first : first + half, :] = mm(left_ref[rs, :], right).astype(BF)


def attn_bwd_kernel(dh, extra, done, need, pos_ref, win_ref, proj_ref, att_ref, g_ref, lse_ref, segr_ref, segc_ref, nT_ref, *refs):
    if extra:
        more_keep_ref, more_send_ref = refs[:2]
        refs = refs[2:]
    dproj_ref, keep_ref, send_ref, sums_ref, dk_ref, dv_ref, dqT_ref = refs
    length, width = att_ref.shape
    heads = width // dh
    scale = 1.0 / math.sqrt(dh)
    dk_ref[...] = jnp.zeros_like(dk_ref)
    dv_ref[...] = jnp.zeros_like(dv_ref)
    row = lax.broadcasted_iota(jnp.int32, (8, width), 0)
    col = lax.broadcasted_iota(jnp.int32, (8, width), 1) // dh
    pick = jnp.where(row == col, 1.0, 0.0).astype(BF)

    def queries(step, _):
        at = rows_of(step)
        q = (proj_ref[at, 0:width].astype(F32) * scale).astype(BF)
        g = g_ref[at, :]
        qall = by_head(q, dh)
        gall = by_head(g, dh)
        og = att_ref[at, :].astype(F32) * g.astype(F32)
        high = og.astype(BF)
        low = (og - high.astype(F32)).astype(BF)
        delta = mm(pick, high, NT) + mm(pick, low, NT)
        delta = jnp.concatenate([delta[h : h + 1, :] for h in range(heads)], axis=1)
        lse = lse_ref[:, rows_of(step, heads * BLK)]
        segq = jnp.concatenate([segr_ref[:, at]] * heads, axis=1)
        dqT_ref[...] = jnp.zeros_like(dqT_ref)
        start = win_ref[0, step]

        def tile(j, _):
            ks = pl.ds(pl.multiple_of(start + j * BLK, 16), BLK)
            kt = proj_ref[ks, width : 2 * width]
            vt = proj_ref[ks, 2 * width : 3 * width]
            kT = kt.T
            same = segc_ref[ks, :] == segq
            p = jnp.where(same, jnp.exp(mm(kt, qall, NT) - lse), 0.0)
            ds = (p * (mm(vt, gall, NT) - delta)).astype(BF)
            dv_ref[ks, :] += mm(p.astype(BF), gall)
            dk_ref[ks, :] += mm(ds, qall)
            for h in range(heads):
                hs = slice(h * dh, (h + 1) * dh)
                dqT_ref[hs, :] += mm(kT[hs, :], ds[:, h * BLK : (h + 1) * BLK])
            return 0

        lax.fori_loop(0, win_ref[1, step], tile, 0)
        dproj_ref[at, 0:width] = (dqT_ref[...] * scale).astype(BF).T
        return 0

    lax.fori_loop(0, length // BLK, queries, 0)
    dproj_ref[:, width : 2 * width] = dk_ref[...].astype(BF)
    dproj_ref[:, 2 * width :] = dv_ref[...].astype(BF)
    sums_ref[...] = jnp.sum(dproj_ref[...].astype(F32), axis=0, keepdims=True)
    first = 0
    if extra:
        first = more_keep_ref.shape[1]
        keep_ref[:, 0:first, :] = more_keep_ref[...]
        send_ref[:, 0:first, :] = more_send_ref[...]
    done(0)
    split_rows(pos_ref, nT_ref, dproj_ref[...], keep_ref, send_ref, first)


def attn_bwd(dh, pos, win, shards, proj, att, g, lse, segr, segc, nT, extra=()):
    length, width = att.shape
    d = nT.shape[0]
    heads = width // dh
    half = d // shards // 2 + (extra[0].shape[1] if extra else 0)
    return call(
        functools.partial(attn_bwd_kernel, dh, bool(extra)), "attn_bwd",
        (array((length, 3 * width)), array((shards, half, 3 * width)), array((shards, half, 3 * width)), array((1, 3 * width), F32)),
        9 + len(extra), 2, [pltpu.VMEM((length, width), F32), pltpu.VMEM((length, width), F32), pltpu.VMEM((width, BLK), F32)],
        flops=2 * length * d * 3 * width + 5 * length * length * 256 * heads,
        moved=length * (d + 8 * width) * 2, far=(0,),
    )(pos, win, proj, att, g, lse, segr, segc, nT, *extra)


def middle_kernel(done, need, pos_ref, frames_ref, a0, a1, a2, own_ref, near_ref, far_ref, whole_ref,
                  w_ref, middle_ref, n_ref, nT_ref):
    place(w_ref, pos_ref, own_ref, near_ref, far_ref)
    width = a0.shape[1]

    def step(at):
        total = frames_ref[at, :].astype(F32) + whole_ref[6:7, :]
        for g, a in enumerate((a0, a1, a2)):
            total = total + mm(a[at, :], w_ref[g * width : (g + 1) * width, :])
        middle_ref[at, :] = total
        unit, _inv = standardize(total)
        normed = (unit * whole_ref[1:2, :] + whole_ref[3:4, :]).astype(BF)
        n_ref[at, :] = normed
        nT_ref[:, at] = normed.T

    blocks(frames_ref.shape[0], step)


def middle(pos, frames, atts, own, near, far, whole):
    rows, d = frames.shape
    return call(
        middle_kernel, "middle",
        (array((d, d)), array((rows, d), F32), array((rows, d)), array((d, rows))), 9, 1,
        flops=2 * rows * d * d, moved=rows * d * 12, far=(0, 1), cost=0.1,
    )(pos, frames, *atts, own, near, far, whole)


def ffn_kernel(own, apart, fresh, offset, done, need, pos_ref, n_ref, nT_ref, cot_ref, *refs):
    refs = list(refs)
    first, second = refs.pop(0), refs.pop(0)
    if apart:
        first, second = (first, second), (refs.pop(0), refs.pop(0))
    bias_ref = refs.pop(0)
    prev_ref = None if fresh else refs.pop(0)
    act_ref, keep_ref, send_ref, bsum_ref, gn_ref = refs[:5]
    core = pos_ref[1]
    if own:
        up_ref, down_ref = first, second
    else:
        down_ref, up_ref = refs[5], refs[6]
        for ref, t in ((up_ref, 0), (down_ref, 1)):
            size = ref.shape[0] // 2
            ref[pl.ds(pl.multiple_of(core * size, size), size), :] = first[t][...]
            ref[pl.ds(pl.multiple_of((1 - core) * size, size), size), :] = second[t][...]
    d = n_ref.shape[1]
    chunk = act_ref.shape[1]

    if not own:
        done(5)
    up = up_ref[:, offset : offset + chunk]
    down = down_ref[offset : offset + chunk, :]
    acts, ghs = [], []
    for i in range(n_ref.shape[0] // BLK):
        at = slice(i * BLK, (i + 1) * BLK)
        hidden = mm(n_ref[at, :], up) + bias_ref[...]
        grad = mm(cot_ref[at, :], down, NT)
        phi = 0.5 + 0.5 * lax.erf(hidden * (1.0 / math.sqrt(2.0)))
        bell = jnp.exp(hidden * hidden * -0.5) * (1.0 / math.sqrt(2.0 * math.pi))
        act = (hidden * phi).astype(BF)
        gh = (grad * (phi + hidden * bell)).astype(BF)
        act_ref[at, :] = act
        base = jnp.zeros((BLK, d), F32) if fresh else prev_ref[at, :]
        gn_ref[at, :] = base + mm(gh, up, NT)
        acts.append(act)
        ghs.append(gh)
    done(0)
    act = jnp.concatenate(acts, axis=0)
    gh = jnp.concatenate(ghs, axis=0)
    bsum_ref[...] = jnp.sum(gh.astype(F32), axis=0, keepdims=True)
    d_down = mm(act, cot_ref[...], TN).astype(BF)
    d_up = mm(nT_ref[...], gh).astype(BF)
    if d > chunk:
        d_up = jnp.concatenate([d_up[r * chunk : (r + 1) * chunk, :] for r in range(d // chunk)], axis=1)
    first = core == 0
    keep_ref[...] = jnp.where(first, d_down, d_up)
    send_ref[...] = jnp.where(first, d_up, d_down)


def ffn(own, offset, pos, n, nT, cot, first, second, bias, grad):
    rows, d = n.shape
    chunk = bias.shape[1]
    fresh = grad is None
    apart = isinstance(first, tuple)
    args = [pos, n, nT, cot, *(first + second if apart else (first, second)), bias] + ([] if fresh else [grad])
    outs = (array((rows, chunk)), array((chunk, d)), array((chunk, d)), array((1, chunk), F32), array((rows, d), F32))
    if not own:
        outs = outs + (array((chunk, d)),)
    return call(
        functools.partial(ffn_kernel, own, apart, fresh, offset), "ffn", outs,
        len(args), 1, [] if own else [pltpu.VMEM((d, chunk), BF)], flops=10 * rows * d * chunk,
        moved=rows * d * 20,
        far=(0,) if own else (0, 5), limit=20 << 20,
    )(*args)


def turn_kernel(done, need, pos_ref, gn_ref, middle_ref, cot_ref, whole_ref, w_ref, t0, t1, t2,
                gm_ref, g0, g1, g2, keep_ref, send_ref, sums_ref, branch_ref, mixT_ref):
    width = g0.shape[1]
    sums_ref[...] = jnp.zeros_like(sums_ref)
    for g, t in enumerate((t0, t1, t2)):
        mixT_ref[g * width : (g + 1) * width, :] = t[...]

    def step(at):
        gn = gn_ref[at, :]
        unit, inverse = standardize(middle_ref[at, :])
        e = gn * whole_ref[1:2, :]
        gm = cot_ref[at, :].astype(F32) + inverse * (
            e - jnp.mean(e, axis=1, keepdims=True) - unit * jnp.mean(e * unit, axis=1, keepdims=True)
        )
        gm_ref[at, :] = gm
        branch = gm.astype(BF)
        branch_ref[at, :] = branch
        sums_ref[0:1, :] += jnp.sum(gn * unit, axis=0, keepdims=True)
        sums_ref[1:2, :] += jnp.sum(gn, axis=0, keepdims=True)
        sums_ref[2:3, :] += jnp.sum(branch.astype(F32), axis=0, keepdims=True)
        for g, out in enumerate((g0, g1, g2)):
            out[at, :] = mm(branch, w_ref[g * width : (g + 1) * width, :], NT).astype(BF)

    blocks(gn_ref.shape[0], step)
    split_rows(pos_ref, mixT_ref, branch_ref[...], keep_ref, send_ref, 0)


def turn(pos, shards, gn, mid, cot, whole, w, attTs):
    rows, d = gn.shape
    width = d // GROUPS
    return call(
        turn_kernel, "turn",
        (array((rows, d), F32),) + (array((rows, width)),) * 3 + (array((shards, d // shards // 2, d)),) * 2 + (array((8, d), F32),),
        9, 1, [pltpu.VMEM((rows, d), BF), pltpu.VMEM((d, rows), BF)],
        flops=4 * rows * d * d, moved=rows * d * 20,
    )(pos, gn, mid, cot, whole, w, *attTs)


def leave_kernel(shards, ups, done, need, pos_ref, frames_ref, gm_ref, whole_ref, p0, p1, p2, w0, w1, w2, two_ref, cot_ref, *refs):
    qv_refs, up_refs, (out_ref, small_ref, tall_ref) = refs[:GROUPS], refs[GROUPS : GROUPS + ups], refs[GROUPS + ups :]
    tall_ref[...] = jnp.zeros_like(tall_ref)

    def step(at):
        gn = 0.0
        for i, (p, w) in enumerate(((p0, w0), (p1, w1), (p2, w2))):
            need(4 + i)
            need(7 + i)
            gn = gn + mm(p[at, :], w[...], NT)
        unit, inverse = standardize(frames_ref[at, :].astype(F32))
        e = gn * whole_ref[0:1, :]
        out_ref[at, :] = gm_ref[at, :] + inverse * (
            e - jnp.mean(e, axis=1, keepdims=True) - unit * jnp.mean(e * unit, axis=1, keepdims=True)
        )
        tall_ref[0:1, :] += jnp.sum(gn * unit, axis=0, keepdims=True)
        tall_ref[2:3, :] += jnp.sum(gn, axis=0, keepdims=True)

    blocks(frames_ref.shape[0], step)
    tall_ref[1:2, :] = two_ref[0:1, :]
    tall_ref[3:4, :] = two_ref[1:2, :]
    tall_ref[6:7, :] = two_ref[2:3, :]
    tall_ref[7:8, :] = cot_ref[...]
    for g, ref in enumerate(qv_refs):
        width = ref.shape[1] // 3
        cols = slice(g * width, (g + 1) * width)
        tall_ref[4:5, cols] = ref[:, 0:width]
        tall_ref[5:6, cols] = ref[:, 2 * width :]
    size = tall_ref.shape[1] // shards
    for k in range(shards):
        want = jnp.bitwise_xor(pos_ref[0], k)
        value = jnp.zeros((8, size), F32)
        for j in range(shards):
            value = jnp.where(want == j, tall_ref[:, j * size : (j + 1) * size], value)
        small_ref[k, 0:8, :] = value
        row = 8
        for ref in up_refs[k * ups // shards : (k + 1) * ups // shards]:
            for c in range(ref.shape[1] // size):
                small_ref[k, row : row + 1, :] = ref[:, c * size : (c + 1) * size]
                row += 1


def leave(pos, shards, frames, gm, whole, dprojs, ws, two, cot_sum, qvs, ups):
    rows, d = frames.shape
    return call(
        functools.partial(leave_kernel, shards, len(ups)), "leave",
        (array((rows, d), F32), array((shards, 12, d // shards), F32)), 12 + len(qvs) + len(ups), 1,
        [pltpu.VMEM((8, d), F32)], flops=6 * rows * d * d, moved=rows * d * 16, far=(0,),
        fetch={4 + i: array(v.shape) for i, v in enumerate((*dprojs, *ws))}, limit=30 << 20,
    )(pos, frames, gm, whole, *dprojs, *ws, two, cot_sum, *qvs, *ups)


def result_kernel(n, offsets, done, need, middle_ref, whole_ref, *refs):
    acts, downs, out_ref = refs[:n], refs[n : 2 * n], refs[2 * n]
    need(0)

    def step(at):
        total = middle_ref[at, :] + whole_ref[7:8, :]
        for i, (a, w, offset) in enumerate(zip(acts, downs, offsets)):
            need(2 + i)
            need(2 + n + i)
            total = total + mm(a[at, :], w[offset : offset + a.shape[1], :])
        out_ref[at, :] = total.astype(BF)

    blocks(middle_ref.shape[0], step)


def result(mid, whole, acts, downs, offsets):
    rows, d = mid.shape
    n = len(acts)
    fetch = {0: array(mid.shape, F32)}
    fetch.update({2 + i: array(v.shape) for i, v in enumerate((*acts, *downs))})
    return call(
        functools.partial(result_kernel, n, offsets), "result", array((rows, d)), 2 + 2 * n, 0,
        flops=2 * rows * d * n * acts[0].shape[1], moved=rows * d * 14, far=(0,), fetch=fetch, limit=36 << 20,
    )(mid, whole, *acts, *downs)


def swap(value, axis, size, bit):
    return lax.ppermute(value, axis, [(i, i ^ bit) for i in range(size)])


def after(value, *others):
    return lax.optimization_barrier((value, *others))[0]


def total(terms):
    out = terms[0].astype(F32)
    for t in terms[1:]:
        out = out + t.astype(F32)
    return out.astype(terms[0].dtype)


def bits_of(size):
    return [1 << b for b in range(size.bit_length() - 1)]


def spread(own, shards):
    stack = own[None]
    for bit in bits_of(shards):
        stack = jnp.concatenate([stack, swap(stack, "shard", shards, bit)], axis=0)
    return stack


def others(own, shards):
    return swap(own, "shard", 2, 1)[None] if shards == 2 else spread(own, shards)[1:]


class Order:
    def __init__(self):
        self.token = None
        self.pins = []

    def land(self, *values):
        if self.token is not None:
            values = lax.optimization_barrier((*values, self.token))[:-1]
        self.pins += values
        return values[0] if len(values) == 1 else values

    def hold(self, *values):
        self.pins += values
        return values[0] if len(values) == 1 else values

    def run(self, kernel, value, token):
        if self.pins or self.token is not None:
            value = after(value, *self.pins, *([] if self.token is None else [self.token]))
        self.pins = []
        out = kernel(value)
        self.token = out[token]
        return out


def combine_kernel(groups, done, need, flag_ref, *refs):
    outs = list(refs[sum(len(terms) for terms, _ in groups) :])
    at = 0
    for terms, cut in groups:
        ins = refs[at : at + len(terms)]
        at += len(terms)

        def summed(rs):
            out = 0.0
            for ref, lead in zip(ins, terms):
                out = out + (ref[rs, :] if lead is None else ref[lead, rs, :]).astype(F32)
            return out

        if cut:
            send, keep = outs.pop(0), outs.pop(0)
            rows = send.shape[0]
            for ref, half in ((send, 1 - flag_ref[0]), (keep, flag_ref[0])):
                ref[...] = summed(pl.ds(pl.multiple_of(half * rows, rows), rows)).astype(ref.dtype)
        else:
            out = outs.pop(0)
            out[...] = summed(slice(None)).astype(out.dtype)


def combine(flag, groups):
    terms, spec, outs = [], [], []
    for group, cut in groups:
        group = [t if isinstance(t, tuple) else (t, None) for t in group]
        terms += [t for t, _ in group]
        spec.append(([lead for _, lead in group], cut))
        rows, cols = group[0][0].shape[-2:]
        outs += [array((rows // 2, cols), group[0][0].dtype)] * 2 if cut else [array((rows, cols), group[0][0].dtype)]
    return call(
        functools.partial(combine_kernel, spec), "combine", tuple(outs), 1 + len(terms), 1, flops=1000, limit=6 << 20,
    )(flag, *terms)


def join_kernel(done, need, flag_ref, part_ref, other_ref, out_ref):
    rows = part_ref.shape[0]
    for ref, half in ((part_ref, flag_ref[0]), (other_ref, 1 - flag_ref[0])):
        out_ref[pl.ds(pl.multiple_of(half * rows, rows), rows), :] = ref[...]


def join(flag, part, other):
    rows, cols = part.shape
    return call(join_kernel, "join", array((2 * rows, cols), part.dtype), 3, 1, flops=1000, limit=6 << 20)(flag, part, other)[0]


class Ring:
    def __init__(self, shards, replicas, order):
        self.shards, self.replicas, self.order = shards, replicas, order
        self.bits = bits_of(replicas)[1:]
        replica = lax.axis_index("replica")
        self.flags = {bit: ((replica // bit) % 2).astype(jnp.int32)[None] for bit in bits_of(replicas)}

    def swap(self, value, bit):
        return swap(value, "replica", self.replicas, bit)

    def total(self, terms):
        return combine(self.flags[1], [(terms, False)])[0] if len(terms) > 1 else terms[0]

    def to_shard(self, pieces):
        for bit in reversed(bits_of(self.shards)):
            if bit == 1:
                send = self.order.hold(self.total(pieces[1]))
                return pieces[0], swap(send, "shard", self.shards, bit)
            send = self.order.hold(jnp.stack([self.total(p) for p in pieces[bit:]]))
            got = swap(send, "shard", self.shards, bit)
            pieces = [p + [(got, k)] for k, p in enumerate(pieces[:bit])]

    def to_halves(self, chunks, bit):
        outs = combine(self.flags[bit], [(terms, True) for terms in chunks])
        self.order.hold(*outs)
        return [([outs[2 * i + 1]], self.swap(outs[2 * i], bit)) for i in range(len(chunks))]

    def to_half(self, terms, bit):
        return self.to_halves([terms], bit)[0]

    def whole(self, part, bit):
        return join(self.flags[bit], part, self.swap(part, bit))

    def both(self, part, bit):
        return self.total([part, self.swap(part, bit)])


def local(replicas, shards, frames, cotangent, segment_ids, norm_gain, norm_bias, w_qkv, qv_bias, w_out, out_bias,
          w_up, up_bias, w_down):
    rows, d = frames.shape
    dh = d // H
    group = d // GROUPS
    hid = up_bias.shape[0]
    chunks = max(1, hid // d)
    chunk = hid // chunks
    shard = lax.axis_index("shard")
    core = lax.axis_index("replica") % 2
    pos = jnp.stack([shard, core]).astype(jnp.int32)
    order = Order()
    ring = Ring(shards, replicas, order)
    run, land, hold = order.run, order.land, order.hold
    twin = lambda v: ring.swap(v, 1)
    win = windows(segment_ids)
    segc = segment_ids.reshape(rows, 1)
    bias_own = up_bias.reshape(1, hid)

    small = jnp.concatenate([norm_gain, norm_bias, qv_bias, out_bias], axis=0)
    small_far = others(small, shards)
    packed = run(lambda v: pack(pos, v), w_qkv, 0)
    qkv_own = packed[GROUPS:]
    near = [others(packed[0], shards)]
    bias_far = others(bias_own, shards)
    more = run(lambda v: pack_more(pos, v, w_up, w_down, chunks), w_out, 0)
    pairs = [(more[1 + 2 * i], more[2 + 2 * i]) for i in range(chunks)]
    if chunk == d:
        pairs = [(jnp.stack(p),) for p in pairs]
    small_far = land(small_far)
    bias_far = land(bias_far)
    normed, normedT, cot_sum, whole, *qv = run(lambda v: enter(pos, v, cotangent, small, small_far), frames, 2)
    near[0] = land(near[0])
    far = [land(twin(near[0]))]
    near += [others(after(packed[g], near[0]), shards) for g in range(1, GROUPS)]

    ws, projs, atts, attTs, lses = [], [], [], [], []
    for g in range(GROUPS):
        w, proj, att, attT, lse = run(
            lambda v: attn_fwd(dh, pos, win, v, qkv_own[g], near[g], far[g], qv[g], segment_ids, segc), normed, 4)
        ws.append(w)
        projs.append(proj)
        atts.append(att)
        attTs.append(attT)
        lses.append(lse)
        if g == 0:
            near[1:] = land(*near[1:])
            far += land(*[twin(v) for v in near[1:]])
            near_out = others(after(more[0], near[1]), shards)
            fetched = [[others(after(v, *far[1:]), shards) for v in pairs[0]]]
        if g == 1:
            fetched += [[others(after(v, lse), shards) for v in pairs[i]] for i in range(1, chunks)]
    near_out = land(near_out)
    far_out = land(twin(near_out))
    w_out_all, mid, n_two, nT_two = run(lambda v: middle(pos, v, atts, w_out, near_out, far_out, whole), frames, 3)

    grad, acts, downs, offsets, up_sums = None, [], [], [], []
    pieces = [[None] * shards for _ in range(chunks)]
    waiting, pending = [], []
    chains, got = [None] * chunks, [None] * chunks
    x = ring.bits[0]
    brought = [None] * chunks
    for k in range(shards):
        for i in range(chunks):
            bias = (bias_own if k == 0 else bias_far[k - 1])[:, i * chunk : (i + 1) * chunk].astype(F32)
            if k == 0:
                out = run(lambda v: ffn(True, i * chunk, pos, v, nT_two, cotangent, w_up, w_down, bias, grad), n_two, 3)
                downs.append(w_down)
                offsets.append(i * chunk)
            else:
                if brought[i] is None:
                    a = [land(v) for v in fetched[i]]
                    brought[i] = a, [land(twin(v)) for v in a]
                elif late[0] is not None:
                    brought[0] = brought[0][0], [land(v) for v in late[0]]
                    late[0] = None
                a, b = [tuple(v[k - 1] for v in half) for half in brought[i]]
                a, b = (a[0], b[0]) if len(a) == 1 else (a, b)
                out = run(lambda v: ffn(False, 0, pos, v, nT_two, cotangent, a, b, bias, grad), n_two, 3)
                downs.append(out[5])
                offsets.append(0)
            if k == 0 and i == 0:
                a = [land(v) for v in fetched[0]]
                late = [[twin(v) for v in a]]
                brought[0] = a, None
            acts.append(out[0])
            up_sums.append(out[3])
            grad = out[4]
            last = k == shards - 1
            if k == 0 and shards == 2:
                pieces[i][k] = [out[1]]
                waiting.append((i, out[2]))
            elif last and i == chunks - 1 and i % 2:
                pieces[i][k] = [out[1]]
                final = twin(hold(out[2]))
                for j, other in pending:
                    pieces[j][0].append(land(other))
                pending = []
                continue
            else:
                pieces[i][k] = [out[1], land(twin(out[2]))]
                early = [(j, twin(after(send, pieces[i][k][1]))) for j, send in waiting]
                for j, other in pending:
                    pieces[j][0].append(land(other))
                waiting, pending = [], early
            if last:
                if i % 2 == 0:
                    chains[i], got[i] = ring.to_shard(pieces[i])
                else:
                    chains[i] = ring.to_halves(pieces[i], x)

    out = run(lambda v: turn(pos, shards, v, mid, cotangent, whole, w_out_all, attTs), grad, 6)
    gm, gs, out_keep, out_send, sums_two = out[0], out[1:4], out[4], out[5], out[6]
    if chunks % 2 == 0:
        pieces[-1][-1].append(land(final))
        chains[-1] = ring.to_halves(pieces[-1], x)
    dprojs, qv_sums, attn = [], [], []

    def back(g, extra=(), go=True):
        dproj, keep, send, sums = run(
            lambda v: attn_bwd(dh, pos, win, shards, projs[g], atts[g], v, lses[g], segment_ids, segc, normedT, extra), gs[g], 3)
        dprojs.append(dproj)
        qv_sums.append(sums)
        return keep, twin(hold(send)) if go else send

    def meet(keep, other):
        other = land(other)
        return ring.to_shard([[(keep, k), (other, k)] for k in range(shards)])

    z, far_bit, *last_bits = ring.bits[1:]
    even, odd = range(0, chunks, 2), range(1, chunks, 2)
    one = back(0, (out_keep, out_send))
    for i in even:
        chains[i], got[i] = ring.to_half(chains[i] + [land(got[i])], x)
    keep, send = back(1, (), False)
    for i in odd:
        chains[i], got[i] = ring.to_shard([keep_ + [land(v)] for keep_, v in chains[i]])
    one, one_got = meet(*one)
    two = back(2, (keep, send))
    for i in (*even, *odd):
        chains[i], got[i] = ring.to_half(chains[i] + [land(got[i])], z)
    d_frames, small_grads = run(
        lambda v: leave(pos, shards, frames, v, whole, dprojs, ws, sums_two, cot_sum, qv_sums, up_sums), gm, 1)
    two, two_got = meet(*two)
    one, one_got = ring.to_half(one + [land(one_got)], x)
    for i in range(chunks):
        chains[i] = hold(ring.total(chains[i] + [land(got[i])]))
        got[i] = ring.swap(chains[i], far_bit)
    out_frames, = run(lambda v: result(v, whole, acts, downs, tuple(offsets)), mid, 0)
    two, two_got = ring.to_half(two + [land(two_got)], x)
    ffn_fulls, attn_fulls = [], []
    for part, other in zip(chains, got):
        part = ring.total([part, land(other)])
        for bit in last_bits:
            part = ring.both(part, bit)
        ffn_fulls.append(ring.whole(ring.whole(part, z), x))
    for terms, other in ((one, one_got), (two, two_got)):
        part = ring.total(terms + [land(other)])
        for bit in ring.bits[1:]:
            part = ring.both(part, bit)
        attn_fulls.append(ring.whole(part, x))
    ffn_grads = []
    for full in ffn_fulls:
        other = twin(full)
        ffn_grads.append((jnp.where(core == 0, full, other), jnp.where(core == 0, other, full)))
    attn_grads = []
    for full in attn_fulls:
        other = twin(full)
        attn_grads.append((jnp.where(core == 0, full, other), jnp.where(core == 0, other, full)))

    if shards == 2:
        vec = ring.total([(small_grads, 0), swap(land(small_grads)[1], "shard", 2, 1)])
    else:
        vec, vec_got = ring.to_shard([[small_grads[k]] for k in range(shards)])
        vec = ring.total(vec + [vec_got])
    for bit in bits_of(replicas):
        vec = ring.both(vec, bit)

    d_down = jnp.concatenate([c[0] for c in ffn_grads], axis=0).astype(F32)
    ups = []
    for c in ffn_grads:
        up = c[1]
        ups.append(jnp.concatenate([up[:, r * chunk : (r + 1) * chunk] for r in range(d // chunk)], axis=0))
    d_up = jnp.concatenate(ups, axis=1).astype(F32)
    half = d // shards // 2
    d_wout = jnp.concatenate([v[:half] for v in attn_grads[0]]).astype(F32)
    groups = [[v[half:] for v in attn_grads[0]], [v[:half] for v in attn_grads[1]], [v[half:] for v in attn_grads[1]]]
    d_qkv = jnp.concatenate([
        jnp.concatenate([g[c][:, t * group : (t + 1) * group] for t in range(3) for g in groups], axis=1)
        for c in range(2)]).astype(F32)
    return (
        out_frames, d_frames, vec[0:2], vec[2:4], d_qkv, vec[4:6], d_wout, vec[6:8], d_up,
        vec[8:].reshape(hid), d_down,
    )


def solution(mesh):
    both = P(("replica", "shard"), None)
    wide, tall, flat = P(None, "shard"), P("shard", None), P("shard")
    return jax.shard_map(
        functools.partial(local, mesh.shape["replica"], mesh.shape["shard"]),
        mesh=mesh,
        in_specs=(both, both, both, wide, wide, tall, wide, tall, wide, wide, flat, tall),
        out_specs=(both, both, wide, wide, tall, wide, tall, wide, wide, flat, tall),
        check_vma=False,
    )
```

```python
import functools
import math

import jax
import jax.numpy as jnp
from jax import lax
from jax.experimental import pallas as pl
from jax.experimental.pallas import tpu as pltpu
from jax.sharding import PartitionSpec as P

H = 12
EPS = 1e-05
NEG = -1e30
F32 = jnp.float32
BF = jnp.bfloat16
NN = (((1,), (0,)), ((), ()))
NT = (((1,), (1,)), ((), ()))
TN = (((0,), (0,)), ((), ()))
BLK = 256
GROUPS = 3
VM = pl.BlockSpec(memory_space=pltpu.VMEM)
SM = pl.BlockSpec(memory_space=pltpu.SMEM)
LIMIT = 14 << 20
ROWS = 512


def mm(a, b, dims=NN):
    return lax.dot_general(a, b, dims, preferred_element_type=F32)


def blocks(rows, body):
    for i in range(rows // ROWS):
        body(slice(i * ROWS, (i + 1) * ROWS))


def rows_of(i, size=BLK):
    return pl.ds(pl.multiple_of(i * size, size), size)


def call(kernel, name, outs, n_in, smem, scratch=(), flops=0, moved=0, far=(), fetch=(), limit=LIMIT, cost=4.0):
    outs = outs if isinstance(outs, tuple) else (outs,)
    fetch = dict(fetch)
    n_out = len(outs)
    scratch = list(scratch)
    n_scratch = len(scratch)
    manual = [outs[i] for i in far] + list(fetch.values())

    def body(*refs):
        ins, rest = list(refs[:n_in]), list(refs[n_in:])
        targets, rest = rest[:n_out], rest[n_out:]
        own, rest = rest[:n_scratch], rest[n_scratch:]
        sem, buffers = rest[-1], rest[:-1]
        reads, writes = {}, {}
        for j, i in enumerate(fetch):
            buffer = buffers[len(far) + j]
            reads[i] = pltpu.make_async_copy(ins[i], buffer, sem.at[len(far) + j])
            reads[i].start()
            ins[i] = buffer
        local_outs = list(targets)
        for j, i in enumerate(far):
            local_outs[i] = buffers[j]

        def done(i):
            writes[i] = pltpu.make_async_copy(buffers[far.index(i)], targets[i], sem.at[far.index(i)])
            writes[i].start()

        def need(i):
            if i in reads:
                reads.pop(i).wait()

        kernel(done, need, *ins, *local_outs, *own)
        for i in far:
            if i not in writes:
                done(i)
        for i in list(reads):
            need(i)
        for copy in writes.values():
            copy.wait()

    hbm = pl.BlockSpec(memory_space=pltpu.HBM)
    out = pl.pallas_call(
        body if manual else functools.partial(kernel, None, None),
        name=name,
        out_shape=tuple(pltpu.HBM(o.shape, o.dtype) if i in far else o for i, o in enumerate(outs)),
        in_specs=[hbm if i in fetch else SM if i < smem else VM for i in range(n_in)],
        out_specs=tuple(hbm if i in far else VM for i in range(n_out)),
        scratch_shapes=scratch + ([pltpu.VMEM(m.shape, m.dtype) for m in manual] + [pltpu.SemaphoreType.DMA((len(manual),))] if manual else []),
        compiler_params=pltpu.CompilerParams(vmem_limit_bytes=limit),
        cost_estimate=pl.CostEstimate(flops=int(flops * cost), bytes_accessed=int(moved * cost), transcendentals=0),
    )
    return out


def array(shape, dtype=BF):
    return jax.ShapeDtypeStruct(shape, dtype)


def standardize(values):
    centered = values - jnp.mean(values, axis=1, keepdims=True)
    inverse = lax.rsqrt(jnp.mean(centered * centered, axis=1, keepdims=True) + EPS)
    return centered * inverse, inverse


def enter_kernel(group, done, need, pos_ref, frames_ref, cot_ref, small_ref, far_ref, normed_ref, normedT_ref, sum_ref, whole_ref, *bias_refs):
    shard = pos_ref[0]
    size = small_ref.shape[1]
    shards = far_ref.shape[0] + 1
    for j in range(shards):
        value = jnp.where(shard == j, small_ref[...].astype(F32), 0.0)
        for k in range(1, shards):
            value = jnp.where(jnp.bitwise_xor(shard, k) == j, far_ref[k - 1].astype(F32), value)
        whole_ref[:, j * size : (j + 1) * size] = value
    for g, ref in enumerate(bias_refs):
        cols = slice(g * group, (g + 1) * group)
        ref[:, 0:group] = whole_ref[4:5, cols]
        ref[:, group : 2 * group] = jnp.zeros((1, group), F32)
        ref[:, 2 * group : 3 * group] = whole_ref[5:6, cols]
    sum_ref[...] = jnp.zeros_like(sum_ref)

    def step(at):
        unit, _inv = standardize(frames_ref[at, :].astype(F32))
        normed = (unit * whole_ref[0:1, :] + whole_ref[2:3, :]).astype(BF)
        normed_ref[at, :] = normed
        normedT_ref[:, at] = normed.T
        sum_ref[...] += jnp.sum(cot_ref[at, :].astype(F32), axis=0, keepdims=True)

    blocks(frames_ref.shape[0], step)


def enter(pos, frames, cot, small, far):
    rows, width = frames.shape
    group = width // GROUPS
    outs = (array((rows, width)), array((width, rows)), array((1, width), F32), array((8, width), F32))
    return call(
        functools.partial(enter_kernel, group), "enter", outs + (array((1, 3 * group), F32),) * GROUPS, 5, 1,
        flops=rows * width * 20, moved=rows * width * 8, far=(1,),
    )(pos, frames, cot, small, far)


def pack_kernel(group, done, need, pos_ref, w_ref, *outs):
    half = w_ref.shape[0] // 2
    d = group * GROUPS
    at = pl.ds(pl.multiple_of(pos_ref[1] * half, half), half)
    for g in range(GROUPS):
        for t in range(3):
            cols = slice(t * d + g * group, t * d + (g + 1) * group)
            to = slice(t * group, (t + 1) * group)
            outs[g][:, to] = w_ref[at, cols]
            outs[GROUPS + g][:, to] = w_ref[:, cols]


def pack(pos, w):
    rows, cols = w.shape
    group = cols // 3 // GROUPS
    return call(
        functools.partial(pack_kernel, group), "pack",
        (array((rows // 2, 3 * group)),) * GROUPS + (array((rows, 3 * group)),) * GROUPS, 2, 1, moved=rows * cols * 5,
    )(pos, w)


def pack_more_kernel(done, need, pos_ref, out_ref, up_ref, down_ref, half_ref, *outs):
    core = pos_ref[1]
    half = half_ref.shape[0]
    half_ref[...] = out_ref[pl.ds(pl.multiple_of(core * half, half), half), :]
    chunks = len(outs) // 2
    up_rows, down_rows = up_ref.shape[0] // 2, down_ref.shape[0] // chunks // 2
    chunk = 2 * down_rows
    for i in range(chunks):
        at = pl.ds(pl.multiple_of(core * up_rows, up_rows), up_rows)
        outs[2 * i][...] = up_ref[at, i * chunk : (i + 1) * chunk]
        at = pl.ds(pl.multiple_of(i * chunk + core * down_rows, down_rows), down_rows)
        outs[2 * i + 1][...] = down_ref[at, :]


def pack_more(pos, w_out, w_up, w_down, chunks):
    d, hid = w_up.shape
    chunk = hid // chunks
    return call(
        pack_more_kernel, "pack_more",
        (array((w_out.shape[0] // 2, d)),) + (array((d // 2, chunk)), array((chunk // 2, d))) * chunks, 4, 1,
        moved=d * hid * 6,
    )(pos, w_out, w_up, w_down)


def windows(seg):
    length = seg.shape[1]
    first = seg[0, ::BLK]
    last = seg[0, BLK - 1 :: BLK]
    begin = jnp.sum((seg < first[:, None]).astype(jnp.int32), axis=1)
    end = jnp.sum((seg <= last[:, None]).astype(jnp.int32), axis=1)
    begin = begin // 16 * 16
    count = (end - begin + BLK - 1) // BLK
    begin = jnp.minimum(begin, length - count * BLK)
    return jnp.stack([begin, count]).astype(jnp.int32)


def by_head(block, dh):
    width = block.shape[1]
    lane = lax.broadcasted_iota(jnp.int32, (1, width), 1) // dh
    zero = jnp.zeros_like(block)
    return jnp.concatenate([jnp.where(lane == h, block, zero) for h in range(width // dh)], axis=0)


def place(full_ref, pos_ref, own_ref, near_ref, far_ref):
    shard, core = pos_ref[0], pos_ref[1]
    size = own_ref.shape[0]
    half = size // 2
    full_ref[pl.ds(pl.multiple_of(shard * size, half), size), :] = own_ref[...]
    for k in range(near_ref.shape[0]):
        base = jnp.bitwise_xor(shard, k + 1) * size
        full_ref[pl.ds(pl.multiple_of(base + core * half, half), half), :] = near_ref[k]
        full_ref[pl.ds(pl.multiple_of(base + (1 - core) * half, half), half), :] = far_ref[k]


def attn_fwd_kernel(dh, done, need, pos_ref, win_ref, normed_ref, own_ref, near_ref, far_ref, bias_ref, segr_ref, segc_ref,
                    w_ref, proj_ref, att_ref, attT_ref, lse_ref, acc_ref):
    width = att_ref.shape[1]
    heads = width // dh
    length = normed_ref.shape[0]
    place(w_ref, pos_ref, own_ref, near_ref, far_ref)

    def project(i, _):
        at = rows_of(i)
        proj_ref[at, :] = (mm(normed_ref[at, :], w_ref[...]) + bias_ref[...]).astype(BF)
        return 0

    lax.fori_loop(0, length // BLK, project, 0)
    done(0)
    done(1)

    def queries(step, _):
        at = rows_of(step)
        q = (proj_ref[at, 0:width].astype(F32) * (1.0 / math.sqrt(dh))).astype(BF)
        qall = by_head(q, dh)
        segq = jnp.concatenate([segr_ref[:, at]] * heads, axis=1)
        acc_ref[...] = jnp.zeros_like(acc_ref)
        start = win_ref[0, step]

        def tile(j, carry):
            m_old, mass = carry
            ks = pl.ds(pl.multiple_of(start + j * BLK, 16), BLK)
            vT = proj_ref[ks, 2 * width : 3 * width].T
            same = segc_ref[ks, :] == segq
            s = jnp.where(same, mm(proj_ref[ks, width : 2 * width], qall, NT), NEG)
            m_new = jnp.maximum(m_old, jnp.max(s, axis=0, keepdims=True))
            p = jnp.exp(s - m_new)
            alpha = jnp.exp(m_old - m_new)
            mass = mass * alpha + jnp.sum(p, axis=0, keepdims=True)
            pb = p.astype(BF)
            for h in range(heads):
                hs, cs = slice(h * dh, (h + 1) * dh), slice(h * BLK, (h + 1) * BLK)
                acc_ref[hs, :] = acc_ref[hs, :] * alpha[:, cs] + mm(vT[hs, :], pb[:, cs])
            return m_new, mass

        carry = (jnp.full((1, heads * BLK), NEG, F32), jnp.zeros((1, heads * BLK), F32))
        peak, mass = lax.fori_loop(0, win_ref[1, step], tile, carry)
        lse_ref[:, rows_of(step, heads * BLK)] = peak + jnp.log(mass)
        outs = []
        for h in range(heads):
            outs.append((acc_ref[h * dh : (h + 1) * dh, :] / mass[:, h * BLK : (h + 1) * BLK]).astype(BF))
        oT = jnp.concatenate(outs, axis=0)
        attT_ref[:, at] = oT
        att_ref[at, :] = oT.T
        return 0

    lax.fori_loop(0, length // BLK, queries, 0)


def attn_fwd(dh, pos, win, normed, own, near, far, bias, segr, segc):
    length, d = normed.shape
    width = own.shape[1] // 3
    heads = width // dh
    return call(
        functools.partial(attn_fwd_kernel, dh), "attn_fwd",
        (array((d, 3 * width)), array((length, 3 * width)), array((length, width)), array((width, length)),
         array((1, length * heads), F32)),
        9, 2, [pltpu.VMEM((width, BLK), F32)],
        flops=2 * length * d * 3 * width + 2 * length * length * 256 * heads,
        moved=length * (d + 6 * width) * 2, far=(0, 1, 3), cost=0.1,
    )(pos, win, normed, own, near, far, bias, segr, segc)


def split_rows(pos_ref, left_ref, right, keep_ref, send_ref, first):
    shard, core = pos_ref[0], pos_ref[1]
    half = left_ref.shape[0] // keep_ref.shape[0] // 2
    for k in range(keep_ref.shape[0]):
        base = jnp.bitwise_xor(shard, k) * (2 * half)
        for ref, part in ((keep_ref, core), (send_ref, 1 - core)):
            rs = pl.ds(pl.multiple_of(base + part * half, half), half)
            ref[k, first : first + half, :] = mm(left_ref[rs, :], right).astype(BF)


def attn_bwd_kernel(dh, extra, done, need, pos_ref, win_ref, proj_ref, att_ref, g_ref, lse_ref, segr_ref, segc_ref, nT_ref, *refs):
    if extra:
        more_keep_ref, more_send_ref = refs[:2]
        refs = refs[2:]
    dproj_ref, keep_ref, send_ref, sums_ref, dk_ref, dv_ref, dqT_ref = refs
    length, width = att_ref.shape
    heads = width // dh
    scale = 1.0 / math.sqrt(dh)
    dk_ref[...] = jnp.zeros_like(dk_ref)
    dv_ref[...] = jnp.zeros_like(dv_ref)
    row = lax.broadcasted_iota(jnp.int32, (8, width), 0)
    col = lax.broadcasted_iota(jnp.int32, (8, width), 1) // dh
    pick = jnp.where(row == col, 1.0, 0.0).astype(BF)

    def queries(step, _):
        at = rows_of(step)
        q = (proj_ref[at, 0:width].astype(F32) * scale).astype(BF)
        g = g_ref[at, :]
        qall = by_head(q, dh)
        gall = by_head(g, dh)
        og = att_ref[at, :].astype(F32) * g.astype(F32)
        high = og.astype(BF)
        low = (og - high.astype(F32)).astype(BF)
        delta = mm(pick, high, NT) + mm(pick, low, NT)
        delta = jnp.concatenate([delta[h : h + 1, :] for h in range(heads)], axis=1)
        lse = lse_ref[:, rows_of(step, heads * BLK)]
        segq = jnp.concatenate([segr_ref[:, at]] * heads, axis=1)
        dqT_ref[...] = jnp.zeros_like(dqT_ref)
        start = win_ref[0, step]

        def tile(j, _):
            ks = pl.ds(pl.multiple_of(start + j * BLK, 16), BLK)
            kt = proj_ref[ks, width : 2 * width]
            vt = proj_ref[ks, 2 * width : 3 * width]
            kT = kt.T
            same = segc_ref[ks, :] == segq
            p = jnp.where(same, jnp.exp(mm(kt, qall, NT) - lse), 0.0)
            ds = (p * (mm(vt, gall, NT) - delta)).astype(BF)
            dv_ref[ks, :] += mm(p.astype(BF), gall)
            dk_ref[ks, :] += mm(ds, qall)
            for h in range(heads):
                hs = slice(h * dh, (h + 1) * dh)
                dqT_ref[hs, :] += mm(kT[hs, :], ds[:, h * BLK : (h + 1) * BLK])
            return 0

        lax.fori_loop(0, win_ref[1, step], tile, 0)
        dproj_ref[at, 0:width] = (dqT_ref[...] * scale).astype(BF).T
        return 0

    lax.fori_loop(0, length // BLK, queries, 0)
    dproj_ref[:, width : 2 * width] = dk_ref[...].astype(BF)
    dproj_ref[:, 2 * width :] = dv_ref[...].astype(BF)
    sums_ref[...] = jnp.sum(dproj_ref[...].astype(F32), axis=0, keepdims=True)
    first = 0
    if extra:
        first = more_keep_ref.shape[1]
        keep_ref[:, 0:first, :] = more_keep_ref[...]
        send_ref[:, 0:first, :] = more_send_ref[...]
    done(0)
    split_rows(pos_ref, nT_ref, dproj_ref[...], keep_ref, send_ref, first)


def attn_bwd(dh, pos, win, shards, proj, att, g, lse, segr, segc, nT, extra=()):
    length, width = att.shape
    d = nT.shape[0]
    heads = width // dh
    half = d // shards // 2 + (extra[0].shape[1] if extra else 0)
    return call(
        functools.partial(attn_bwd_kernel, dh, bool(extra)), "attn_bwd",
        (array((length, 3 * width)), array((shards, half, 3 * width)), array((shards, half, 3 * width)), array((1, 3 * width), F32)),
        9 + len(extra), 2, [pltpu.VMEM((length, width), F32), pltpu.VMEM((length, width), F32), pltpu.VMEM((width, BLK), F32)],
        flops=2 * length * d * 3 * width + 5 * length * length * 256 * heads,
        moved=length * (d + 8 * width) * 2, far=(0,),
    )(pos, win, proj, att, g, lse, segr, segc, nT, *extra)


def middle_kernel(done, need, pos_ref, frames_ref, a0, a1, a2, own_ref, near_ref, far_ref, whole_ref,
                  w_ref, middle_ref, n_ref, nT_ref):
    place(w_ref, pos_ref, own_ref, near_ref, far_ref)
    width = a0.shape[1]

    def step(at):
        total = frames_ref[at, :].astype(F32) + whole_ref[6:7, :]
        for g, a in enumerate((a0, a1, a2)):
            total = total + mm(a[at, :], w_ref[g * width : (g + 1) * width, :])
        middle_ref[at, :] = total
        unit, _inv = standardize(total)
        normed = (unit * whole_ref[1:2, :] + whole_ref[3:4, :]).astype(BF)
        n_ref[at, :] = normed
        nT_ref[:, at] = normed.T

    blocks(frames_ref.shape[0], step)


def middle(pos, frames, atts, own, near, far, whole):
    rows, d = frames.shape
    return call(
        middle_kernel, "middle",
        (array((d, d)), array((rows, d), F32), array((rows, d)), array((d, rows))), 9, 1,
        flops=2 * rows * d * d, moved=rows * d * 12, far=(0, 1), cost=0.1,
    )(pos, frames, *atts, own, near, far, whole)


def ffn_kernel(own, apart, fresh, offset, done, need, pos_ref, n_ref, nT_ref, cot_ref, *refs):
    refs = list(refs)
    first, second = refs.pop(0), refs.pop(0)
    if apart:
        first, second = (first, second), (refs.pop(0), refs.pop(0))
    bias_ref = refs.pop(0)
    prev_ref = None if fresh else refs.pop(0)
    act_ref, keep_ref, send_ref, bsum_ref, gn_ref = refs[:5]
    core = pos_ref[1]
    if own:
        up_ref, down_ref = first, second
    else:
        down_ref, up_ref = refs[5], refs[6]
        for ref, t in ((up_ref, 0), (down_ref, 1)):
            size = ref.shape[0] // 2
            ref[pl.ds(pl.multiple_of(core * size, size), size), :] = first[t][...]
            ref[pl.ds(pl.multiple_of((1 - core) * size, size), size), :] = second[t][...]
    d = n_ref.shape[1]
    chunk = act_ref.shape[1]

    if not own:
        done(5)
    up = up_ref[:, offset : offset + chunk]
    down = down_ref[offset : offset + chunk, :]
    acts, ghs = [], []
    for i in range(n_ref.shape[0] // BLK):
        at = slice(i * BLK, (i + 1) * BLK)
        hidden = mm(n_ref[at, :], up) + bias_ref[...]
        grad = mm(cot_ref[at, :], down, NT)
        phi = 0.5 + 0.5 * lax.erf(hidden * (1.0 / math.sqrt(2.0)))
        bell = jnp.exp(hidden * hidden * -0.5) * (1.0 / math.sqrt(2.0 * math.pi))
        act = (hidden * phi).astype(BF)
        gh = (grad * (phi + hidden * bell)).astype(BF)
        act_ref[at, :] = act
        base = jnp.zeros((BLK, d), F32) if fresh else prev_ref[at, :]
        gn_ref[at, :] = base + mm(gh, up, NT)
        acts.append(act)
        ghs.append(gh)
    done(0)
    act = jnp.concatenate(acts, axis=0)
    gh = jnp.concatenate(ghs, axis=0)
    bsum_ref[...] = jnp.sum(gh.astype(F32), axis=0, keepdims=True)
    d_down = mm(act, cot_ref[...], TN).astype(BF)
    d_up = mm(nT_ref[...], gh).astype(BF)
    if d > chunk:
        d_up = jnp.concatenate([d_up[r * chunk : (r + 1) * chunk, :] for r in range(d // chunk)], axis=1)
    first = core == 0
    keep_ref[...] = jnp.where(first, d_down, d_up)
    send_ref[...] = jnp.where(first, d_up, d_down)


def ffn(own, offset, pos, n, nT, cot, first, second, bias, grad):
    rows, d = n.shape
    chunk = bias.shape[1]
    fresh = grad is None
    apart = isinstance(first, tuple)
    args = [pos, n, nT, cot, *(first + second if apart else (first, second)), bias] + ([] if fresh else [grad])
    outs = (array((rows, chunk)), array((chunk, d)), array((chunk, d)), array((1, chunk), F32), array((rows, d), F32))
    if not own:
        outs = outs + (array((chunk, d)),)
    return call(
        functools.partial(ffn_kernel, own, apart, fresh, offset), "ffn", outs,
        len(args), 1, [] if own else [pltpu.VMEM((d, chunk), BF)], flops=10 * rows * d * chunk,
        moved=rows * d * 20,
        far=(0,) if own else (0, 5), limit=20 << 20,
    )(*args)


def turn_kernel(done, need, pos_ref, gn_ref, middle_ref, cot_ref, whole_ref, w_ref, t0, t1, t2,
                gm_ref, g0, g1, g2, keep_ref, send_ref, sums_ref, branch_ref, mixT_ref):
    width = g0.shape[1]
    sums_ref[...] = jnp.zeros_like(sums_ref)
    for g, t in enumerate((t0, t1, t2)):
        mixT_ref[g * width : (g + 1) * width, :] = t[...]

    def step(at):
        gn = gn_ref[at, :]
        unit, inverse = standardize(middle_ref[at, :])
        e = gn * whole_ref[1:2, :]
        gm = cot_ref[at, :].astype(F32) + inverse * (
            e - jnp.mean(e, axis=1, keepdims=True) - unit * jnp.mean(e * unit, axis=1, keepdims=True)
        )
        gm_ref[at, :] = gm
        branch = gm.astype(BF)
        branch_ref[at, :] = branch
        sums_ref[0:1, :] += jnp.sum(gn * unit, axis=0, keepdims=True)
        sums_ref[1:2, :] += jnp.sum(gn, axis=0, keepdims=True)
        sums_ref[2:3, :] += jnp.sum(branch.astype(F32), axis=0, keepdims=True)
        for g, out in enumerate((g0, g1, g2)):
            out[at, :] = mm(branch, w_ref[g * width : (g + 1) * width, :], NT).astype(BF)

    blocks(gn_ref.shape[0], step)
    split_rows(pos_ref, mixT_ref, branch_ref[...], keep_ref, send_ref, 0)


def turn(pos, shards, gn, mid, cot, whole, w, attTs):
    rows, d = gn.shape
    width = d // GROUPS
    return call(
        turn_kernel, "turn",
        (array((rows, d), F32),) + (array((rows, width)),) * 3 + (array((shards, d // shards // 2, d)),) * 2 + (array((8, d), F32),),
        9, 1, [pltpu.VMEM((rows, d), BF), pltpu.VMEM((d, rows), BF)],
        flops=4 * rows * d * d, moved=rows * d * 20,
    )(pos, gn, mid, cot, whole, w, *attTs)


def leave_kernel(shards, ups, done, need, pos_ref, frames_ref, gm_ref, whole_ref, p0, p1, p2, w0, w1, w2, two_ref, cot_ref, *refs):
    qv_refs, up_refs, (out_ref, small_ref, tall_ref) = refs[:GROUPS], refs[GROUPS : GROUPS + ups], refs[GROUPS + ups :]
    tall_ref[...] = jnp.zeros_like(tall_ref)

    def step(at):
        gn = 0.0
        for i, (p, w) in enumerate(((p0, w0), (p1, w1), (p2, w2))):
            need(4 + i)
            need(7 + i)
            gn = gn + mm(p[at, :], w[...], NT)
        unit, inverse = standardize(frames_ref[at, :].astype(F32))
        e = gn * whole_ref[0:1, :]
        out_ref[at, :] = gm_ref[at, :] + inverse * (
            e - jnp.mean(e, axis=1, keepdims=True) - unit * jnp.mean(e * unit, axis=1, keepdims=True)
        )
        tall_ref[0:1, :] += jnp.sum(gn * unit, axis=0, keepdims=True)
        tall_ref[2:3, :] += jnp.sum(gn, axis=0, keepdims=True)

    blocks(frames_ref.shape[0], step)
    tall_ref[1:2, :] = two_ref[0:1, :]
    tall_ref[3:4, :] = two_ref[1:2, :]
    tall_ref[6:7, :] = two_ref[2:3, :]
    tall_ref[7:8, :] = cot_ref[...]
    for g, ref in enumerate(qv_refs):
        width = ref.shape[1] // 3
        cols = slice(g * width, (g + 1) * width)
        tall_ref[4:5, cols] = ref[:, 0:width]
        tall_ref[5:6, cols] = ref[:, 2 * width :]
    size = tall_ref.shape[1] // shards
    for k in range(shards):
        want = jnp.bitwise_xor(pos_ref[0], k)
        value = jnp.zeros((8, size), F32)
        for j in range(shards):
            value = jnp.where(want == j, tall_ref[:, j * size : (j + 1) * size], value)
        small_ref[k, 0:8, :] = value
        row = 8
        for ref in up_refs[k * ups // shards : (k + 1) * ups // shards]:
            for c in range(ref.shape[1] // size):
                small_ref[k, row : row + 1, :] = ref[:, c * size : (c + 1) * size]
                row += 1


def leave(pos, shards, frames, gm, whole, dprojs, ws, two, cot_sum, qvs, ups):
    rows, d = frames.shape
    return call(
        functools.partial(leave_kernel, shards, len(ups)), "leave",
        (array((rows, d), F32), array((shards, 12, d // shards), F32)), 12 + len(qvs) + len(ups), 1,
        [pltpu.VMEM((8, d), F32)], flops=6 * rows * d * d, moved=rows * d * 16, far=(0,),
        fetch={4 + i: array(v.shape) for i, v in enumerate((*dprojs, *ws))}, limit=30 << 20,
    )(pos, frames, gm, whole, *dprojs, *ws, two, cot_sum, *qvs, *ups)


def result_kernel(n, offsets, done, need, middle_ref, whole_ref, *refs):
    acts, downs, out_ref = refs[:n], refs[n : 2 * n], refs[2 * n]
    need(0)

    def step(at):
        total = middle_ref[at, :] + whole_ref[7:8, :]
        for i, (a, w, offset) in enumerate(zip(acts, downs, offsets)):
            need(2 + i)
            need(2 + n + i)
            total = total + mm(a[at, :], w[offset : offset + a.shape[1], :])
        out_ref[at, :] = total.astype(BF)

    blocks(middle_ref.shape[0], step)


def result(mid, whole, acts, downs, offsets):
    rows, d = mid.shape
    n = len(acts)
    fetch = {0: array(mid.shape, F32)}
    fetch.update({2 + i: array(v.shape) for i, v in enumerate((*acts, *downs))})
    return call(
        functools.partial(result_kernel, n, offsets), "result", array((rows, d)), 2 + 2 * n, 0,
        flops=2 * rows * d * n * acts[0].shape[1], moved=rows * d * 14, far=(0,), fetch=fetch, limit=36 << 20,
    )(mid, whole, *acts, *downs)


def swap(value, axis, size, bit):
    return lax.ppermute(value, axis, [(i, i ^ bit) for i in range(size)])


def after(value, *others):
    return lax.optimization_barrier((value, *others))[0]


def total(terms):
    out = terms[0].astype(F32)
    for t in terms[1:]:
        out = out + t.astype(F32)
    return out.astype(terms[0].dtype)


def bits_of(size):
    return [1 << b for b in range(size.bit_length() - 1)]


def spread(own, shards):
    stack = own[None]
    for bit in bits_of(shards):
        stack = jnp.concatenate([stack, swap(stack, "shard", shards, bit)], axis=0)
    return stack


def others(own, shards):
    return swap(own, "shard", 2, 1)[None] if shards == 2 else spread(own, shards)[1:]


class Order:
    def __init__(self):
        self.token = None
        self.pins = []

    def land(self, *values):
        if self.token is not None:
            values = lax.optimization_barrier((*values, self.token))[:-1]
        self.pins += values
        return values[0] if len(values) == 1 else values

    def hold(self, *values):
        self.pins += values
        return values[0] if len(values) == 1 else values

    def run(self, kernel, value, token):
        if self.pins or self.token is not None:
            value = after(value, *self.pins, *([] if self.token is None else [self.token]))
        self.pins = []
        out = kernel(value)
        self.token = out[token]
        return out


def combine_kernel(groups, done, need, flag_ref, *refs):
    outs = list(refs[sum(len(terms) for terms, _ in groups) :])
    at = 0
    for terms, cut in groups:
        ins = refs[at : at + len(terms)]
        at += len(terms)

        def summed(rs):
            out = 0.0
            for ref, lead in zip(ins, terms):
                out = out + (ref[rs, :] if lead is None else ref[lead, rs, :]).astype(F32)
            return out

        if cut:
            send, keep = outs.pop(0), outs.pop(0)
            rows = send.shape[0]
            for ref, half in ((send, 1 - flag_ref[0]), (keep, flag_ref[0])):
                ref[...] = summed(pl.ds(pl.multiple_of(half * rows, rows), rows)).astype(ref.dtype)
        else:
            out = outs.pop(0)
            out[...] = summed(slice(None)).astype(out.dtype)


def combine(flag, groups):
    terms, spec, outs = [], [], []
    for group, cut in groups:
        group = [t if isinstance(t, tuple) else (t, None) for t in group]
        terms += [t for t, _ in group]
        spec.append(([lead for _, lead in group], cut))
        rows, cols = group[0][0].shape[-2:]
        outs += [array((rows // 2, cols), group[0][0].dtype)] * 2 if cut else [array((rows, cols), group[0][0].dtype)]
    return call(
        functools.partial(combine_kernel, spec), "combine", tuple(outs), 1 + len(terms), 1, flops=1000, limit=6 << 20,
    )(flag, *terms)


def join_kernel(done, need, flag_ref, part_ref, other_ref, out_ref):
    rows = part_ref.shape[0]
    for ref, half in ((part_ref, flag_ref[0]), (other_ref, 1 - flag_ref[0])):
        out_ref[pl.ds(pl.multiple_of(half * rows, rows), rows), :] = ref[...]


def join(flag, part, other):
    rows, cols = part.shape
    return call(join_kernel, "join", array((2 * rows, cols), part.dtype), 3, 1, flops=1000, limit=6 << 20)(flag, part, other)[0]


class Ring:
    def __init__(self, shards, replicas, order):
        self.shards, self.replicas, self.order = shards, replicas, order
        self.bits = bits_of(replicas)[1:]
        replica = lax.axis_index("replica")
        self.flags = {bit: ((replica // bit) % 2).astype(jnp.int32)[None] for bit in bits_of(replicas)}

    def swap(self, value, bit):
        return swap(value, "replica", self.replicas, bit)

    def total(self, terms):
        return combine(self.flags[1], [(terms, False)])[0] if len(terms) > 1 else terms[0]

    def to_shard(self, pieces):
        for bit in reversed(bits_of(self.shards)):
            if bit == 1:
                send = self.order.hold(self.total(pieces[1]))
                return pieces[0], swap(send, "shard", self.shards, bit)
            send = self.order.hold(jnp.stack([self.total(p) for p in pieces[bit:]]))
            got = swap(send, "shard", self.shards, bit)
            pieces = [p + [(got, k)] for k, p in enumerate(pieces[:bit])]

    def to_halves(self, chunks, bit):
        outs = combine(self.flags[bit], [(terms, True) for terms in chunks])
        self.order.hold(*outs)
        return [([outs[2 * i + 1]], self.swap(outs[2 * i], bit)) for i in range(len(chunks))]

    def to_half(self, terms, bit):
        return self.to_halves([terms], bit)[0]

    def whole(self, part, bit):
        return join(self.flags[bit], part, self.swap(part, bit))

    def both(self, part, bit):
        return self.total([part, self.swap(part, bit)])


def local(replicas, shards, frames, cotangent, segment_ids, norm_gain, norm_bias, w_qkv, qv_bias, w_out, out_bias,
          w_up, up_bias, w_down):
    rows, d = frames.shape
    dh = d // H
    group = d // GROUPS
    hid = up_bias.shape[0]
    chunks = max(1, hid // d)
    chunk = hid // chunks
    shard = lax.axis_index("shard")
    core = lax.axis_index("replica") % 2
    pos = jnp.stack([shard, core]).astype(jnp.int32)
    order = Order()
    ring = Ring(shards, replicas, order)
    run, land, hold = order.run, order.land, order.hold
    twin = lambda v: ring.swap(v, 1)
    win = windows(segment_ids)
    segc = segment_ids.reshape(rows, 1)
    bias_own = up_bias.reshape(1, hid)

    small = jnp.concatenate([norm_gain, norm_bias, qv_bias, out_bias], axis=0)
    small_far = others(small, shards)
    packed = run(lambda v: pack(pos, v), w_qkv, 0)
    qkv_own = packed[GROUPS:]
    near = [others(packed[0], shards)]
    bias_far = others(bias_own, shards)
    more = run(lambda v: pack_more(pos, v, w_up, w_down, chunks), w_out, 0)
    pairs = [(more[1 + 2 * i], more[2 + 2 * i]) for i in range(chunks)]
    if chunk == d:
        pairs = [(jnp.stack(p),) for p in pairs]
    small_far = land(small_far)
    bias_far = land(bias_far)
    normed, normedT, cot_sum, whole, *qv = run(lambda v: enter(pos, v, cotangent, small, small_far), frames, 2)
    near[0] = land(near[0])
    far = [land(twin(near[0]))]
    near += [others(after(packed[g], near[0]), shards) for g in range(1, GROUPS)]

    ws, projs, atts, attTs, lses = [], [], [], [], []
    for g in range(GROUPS):
        w, proj, att, attT, lse = run(
            lambda v: attn_fwd(dh, pos, win, v, qkv_own[g], near[g], far[g], qv[g], segment_ids, segc), normed, 4)
        ws.append(w)
        projs.append(proj)
        atts.append(att)
        attTs.append(attT)
        lses.append(lse)
        if g == 0:
            near[1:] = land(*near[1:])
            far += land(*[twin(v) for v in near[1:]])
            near_out = others(after(more[0], near[1]), shards)
            fetched = [[others(after(v, *far[1:]), shards) for v in pairs[0]]]
        if g == 1:
            fetched += [[others(after(v, lse), shards) for v in pairs[i]] for i in range(1, chunks)]
    near_out = land(near_out)
    far_out = land(twin(near_out))
    w_out_all, mid, n_two, nT_two = run(lambda v: middle(pos, v, atts, w_out, near_out, far_out, whole), frames, 3)

    grad, acts, downs, offsets, up_sums = None, [], [], [], []
    pieces = [[None] * shards for _ in range(chunks)]
    waiting, pending = [], []
    chains, got = [None] * chunks, [None] * chunks
    x = ring.bits[0]
    brought = [None] * chunks
    for k in range(shards):
        for i in range(chunks):
            bias = (bias_own if k == 0 else bias_far[k - 1])[:, i * chunk : (i + 1) * chunk].astype(F32)
            if k == 0:
                out = run(lambda v: ffn(True, i * chunk, pos, v, nT_two, cotangent, w_up, w_down, bias, grad), n_two, 3)
                downs.append(w_down)
                offsets.append(i * chunk)
            else:
                if brought[i] is None:
                    a = [land(v) for v in fetched[i]]
                    brought[i] = a, [land(twin(v)) for v in a]
                elif late[0] is not None:
                    brought[0] = brought[0][0], [land(v) for v in late[0]]
                    late[0] = None
                a, b = [tuple(v[k - 1] for v in half) for half in brought[i]]
                a, b = (a[0], b[0]) if len(a) == 1 else (a, b)
                out = run(lambda v: ffn(False, 0, pos, v, nT_two, cotangent, a, b, bias, grad), n_two, 3)
                downs.append(out[5])
                offsets.append(0)
            if k == 0 and i == 0:
                a = [land(v) for v in fetched[0]]
                late = [[twin(v) for v in a]]
                brought[0] = a, None
            acts.append(out[0])
            up_sums.append(out[3])
            grad = out[4]
            last = k == shards - 1
            if k == 0 and shards == 2:
                pieces[i][k] = [out[1]]
                waiting.append((i, out[2]))
            elif last and i == chunks - 1 and i % 2:
                pieces[i][k] = [out[1]]
                final = twin(hold(out[2]))
                for j, other in pending:
                    pieces[j][0].append(land(other))
                pending = []
                continue
            else:
                pieces[i][k] = [out[1], land(twin(out[2]))]
                early = [(j, twin(after(send, pieces[i][k][1]))) for j, send in waiting]
                for j, other in pending:
                    pieces[j][0].append(land(other))
                waiting, pending = [], early
            if last:
                if i % 2 == 0:
                    chains[i], got[i] = ring.to_shard(pieces[i])
                else:
                    chains[i] = ring.to_halves(pieces[i], x)

    out = run(lambda v: turn(pos, shards, v, mid, cotangent, whole, w_out_all, attTs), grad, 6)
    gm, gs, out_keep, out_send, sums_two = out[0], out[1:4], out[4], out[5], out[6]
    if chunks % 2 == 0:
        pieces[-1][-1].append(land(final))
        chains[-1] = ring.to_halves(pieces[-1], x)
    dprojs, qv_sums, attn = [], [], []

    def back(g, extra=(), go=True):
        dproj, keep, send, sums = run(
            lambda v: attn_bwd(dh, pos, win, shards, projs[g], atts[g], v, lses[g], segment_ids, segc, normedT, extra), gs[g], 3)
        dprojs.append(dproj)
        qv_sums.append(sums)
        return keep, twin(hold(send)) if go else send

    def meet(keep, other):
        other = land(other)
        return ring.to_shard([[(keep, k), (other, k)] for k in range(shards)])

    z, far_bit, *last_bits = ring.bits[1:]
    even, odd = range(0, chunks, 2), range(1, chunks, 2)
    one = back(0, (out_keep, out_send))
    for i in even:
        chains[i], got[i] = ring.to_half(chains[i] + [land(got[i])], x)
    keep, send = back(1, (), False)
    for i in odd:
        chains[i], got[i] = ring.to_shard([keep_ + [land(v)] for keep_, v in chains[i]])
    one, one_got = meet(*one)
    two = back(2, (keep, send))
    for i in (*even, *odd):
        chains[i], got[i] = ring.to_half(chains[i] + [land(got[i])], z)
    d_frames, small_grads = run(
        lambda v: leave(pos, shards, frames, v, whole, dprojs, ws, sums_two, cot_sum, qv_sums, up_sums), gm, 1)
    two, two_got = meet(*two)
    one, one_got = ring.to_half(one + [land(one_got)], x)
    for i in range(chunks):
        chains[i] = hold(ring.total(chains[i] + [land(got[i])]))
        got[i] = ring.swap(chains[i], far_bit)
        order.token = chains[i]
    small, small_got = ring.to_shard([[small_grads[k]] for k in range(shards)])
    small = hold(ring.total(small + [land(small_got)]))
    small_got = ring.swap(small, x)
    out_frames, = run(lambda v: result(v, whole, acts, downs, tuple(offsets)), mid, 0)

    def add_step(part, other):
        order.token = ring.total([*part, after(other, order.token)])
        return order.token

    def join_step(part, other, bit):
        order.token = join(ring.flags[bit], part, after(other, order.token))
        return order.token

    full, wait = [None] * chunks, [None] * chunks

    def add_far(i):
        full[i] = add_step([chains[i]], got[i])
        for bit in last_bits:
            full[i] = add_step([full[i]], ring.swap(full[i], bit))
        wait[i] = ring.swap(full[i], z)

    def join_next(i, bit, next_bit):
        full[i] = join_step(full[i], wait[i], bit)
        wait[i] = ring.swap(full[i], next_bit)

    tail = range(1, chunks)
    small = add_step([small], small_got)
    small_got = ring.swap(small, z)
    add_far(0)
    one = add_step(one, one_got)
    one_got = ring.swap(one, z)
    send, keep = combine(ring.flags[x], [([*two, after(two_got, order.token)], True)])
    order.token = send
    two_got = ring.swap(send, x)
    for i in tail:
        add_far(i)
    join_next(0, z, x)
    small = add_step([small], small_got)
    small_got = ring.swap(small, 1)
    one = add_step([one], one_got)
    one_got = ring.swap(one, far_bit)
    small = add_step([small], small_got)
    small_got = ring.swap(small, far_bit)
    two = add_step([keep], two_got)
    two_got = ring.swap(two, z)
    for i in tail:
        join_next(i, z, x)
    two = add_step([two], two_got)
    two_got = ring.swap(two, far_bit)
    join_next(0, x, 1)
    one = add_step([one], one_got)
    small = add_step([small], small_got)
    for bit in last_bits:
        one = add_step([one], ring.swap(one, bit))
        small = add_step([small], ring.swap(small, bit))
    one_got = ring.swap(one, x)
    two = add_step([two], two_got)
    for bit in last_bits:
        two = add_step([two], ring.swap(two, bit))
    two_got = ring.swap(two, x)
    for i in tail:
        join_next(i, x, 1)
    one = join_step(one, one_got, x)
    two = join_step(two, two_got, x)
    vec = small
    ffn_grads = [
        (jnp.where(core == 0, mine, other), jnp.where(core == 0, other, mine)) for mine, other in zip(full, wait)]
    attn_grads = []
    for mine in (one, two):
        other = twin(mine)
        attn_grads.append((jnp.where(core == 0, mine, other), jnp.where(core == 0, other, mine)))

    d_down = jnp.concatenate([c[0] for c in ffn_grads], axis=0).astype(F32)
    ups = []
    for c in ffn_grads:
        up = c[1]
        ups.append(jnp.concatenate([up[:, r * chunk : (r + 1) * chunk] for r in range(d // chunk)], axis=0))
    d_up = jnp.concatenate(ups, axis=1).astype(F32)
    half = d // shards // 2
    d_wout = jnp.concatenate([v[:half] for v in attn_grads[0]]).astype(F32)
    groups = [[v[half:] for v in attn_grads[0]], [v[:half] for v in attn_grads[1]], [v[half:] for v in attn_grads[1]]]
    d_qkv = jnp.concatenate([
        jnp.concatenate([g[c][:, t * group : (t + 1) * group] for t in range(3) for g in groups], axis=1)
        for c in range(2)]).astype(F32)
    return (
        out_frames, d_frames, vec[0:2], vec[2:4], d_qkv, vec[4:6], d_wout, vec[6:8], d_up,
        vec[8:].reshape(hid), d_down,
    )


def solution(mesh):
    both = P(("replica", "shard"), None)
    wide, tall, flat = P(None, "shard"), P("shard", None), P("shard")
    return jax.shard_map(
        functools.partial(local, mesh.shape["replica"], mesh.shape["shard"]),
        mesh=mesh,
        in_specs=(both, both, both, wide, wide, tall, wide, tall, wide, wide, flat, tall),
        out_specs=(both, both, wide, wide, tall, wide, tall, wide, wide, flat, tall),
        check_vma=False,
    )
```

```python
import functools
import math

import jax
import jax.numpy as jnp
from jax import lax
from jax.experimental import pallas as pl
from jax.experimental.pallas import tpu as pltpu
from jax.sharding import PartitionSpec as P

H = 12
EPS = 1e-05
NEG = -1e30
F32 = jnp.float32
BF = jnp.bfloat16
NN = (((1,), (0,)), ((), ()))
NT = (((1,), (1,)), ((), ()))
TN = (((0,), (0,)), ((), ()))
BLK = 256
GROUPS = 3
VM = pl.BlockSpec(memory_space=pltpu.VMEM)
SM = pl.BlockSpec(memory_space=pltpu.SMEM)
LIMIT = 14 << 20
ROWS = 512


def mm(a, b, dims=NN):
    return lax.dot_general(a, b, dims, preferred_element_type=F32)


def blocks(rows, body):
    for i in range(rows // ROWS):
        body(slice(i * ROWS, (i + 1) * ROWS))


def rows_of(i, size=BLK):
    return pl.ds(pl.multiple_of(i * size, size), size)


def call(kernel, name, outs, n_in, smem, scratch=(), flops=0, moved=0, far=(), fetch=(), limit=LIMIT, cost=4.0):
    outs = outs if isinstance(outs, tuple) else (outs,)
    fetch = dict(fetch)
    n_out = len(outs)
    scratch = list(scratch)
    n_scratch = len(scratch)
    manual = [outs[i] for i in far] + list(fetch.values())

    def body(*refs):
        ins, rest = list(refs[:n_in]), list(refs[n_in:])
        targets, rest = rest[:n_out], rest[n_out:]
        own, rest = rest[:n_scratch], rest[n_scratch:]
        sem, buffers = rest[-1], rest[:-1]
        reads, writes = {}, {}
        for j, i in enumerate(fetch):
            buffer = buffers[len(far) + j]
            reads[i] = pltpu.make_async_copy(ins[i], buffer, sem.at[len(far) + j])
            reads[i].start()
            ins[i] = buffer
        local_outs = list(targets)
        for j, i in enumerate(far):
            local_outs[i] = buffers[j]

        def done(i):
            writes[i] = pltpu.make_async_copy(buffers[far.index(i)], targets[i], sem.at[far.index(i)])
            writes[i].start()

        def need(i):
            if i in reads:
                reads.pop(i).wait()

        kernel(done, need, *ins, *local_outs, *own)
        for i in far:
            if i not in writes:
                done(i)
        for i in list(reads):
            need(i)
        for copy in writes.values():
            copy.wait()

    hbm = pl.BlockSpec(memory_space=pltpu.HBM)
    out = pl.pallas_call(
        body if manual else functools.partial(kernel, None, None),
        name=name,
        out_shape=tuple(pltpu.HBM(o.shape, o.dtype) if i in far else o for i, o in enumerate(outs)),
        in_specs=[hbm if i in fetch else SM if i < smem else VM for i in range(n_in)],
        out_specs=tuple(hbm if i in far else VM for i in range(n_out)),
        scratch_shapes=scratch + ([pltpu.VMEM(m.shape, m.dtype) for m in manual] + [pltpu.SemaphoreType.DMA((len(manual),))] if manual else []),
        compiler_params=pltpu.CompilerParams(vmem_limit_bytes=limit),
        cost_estimate=pl.CostEstimate(flops=int(flops * cost), bytes_accessed=int(moved * cost), transcendentals=0),
    )
    return out


def array(shape, dtype=BF):
    return jax.ShapeDtypeStruct(shape, dtype)


def standardize(values):
    centered = values - jnp.mean(values, axis=1, keepdims=True)
    inverse = lax.rsqrt(jnp.mean(centered * centered, axis=1, keepdims=True) + EPS)
    return centered * inverse, inverse


def enter_kernel(group, done, need, pos_ref, frames_ref, cot_ref, small_ref, far_ref, normed_ref, normedT_ref, sum_ref, whole_ref, *bias_refs):
    shard = pos_ref[0]
    size = small_ref.shape[1]
    shards = far_ref.shape[0] + 1
    for j in range(shards):
        value = jnp.where(shard == j, small_ref[...].astype(F32), 0.0)
        for k in range(1, shards):
            value = jnp.where(jnp.bitwise_xor(shard, k) == j, far_ref[k - 1].astype(F32), value)
        whole_ref[:, j * size : (j + 1) * size] = value
    for g, ref in enumerate(bias_refs):
        cols = slice(g * group, (g + 1) * group)
        ref[:, 0:group] = whole_ref[4:5, cols]
        ref[:, group : 2 * group] = jnp.zeros((1, group), F32)
        ref[:, 2 * group : 3 * group] = whole_ref[5:6, cols]
    sum_ref[...] = jnp.zeros_like(sum_ref)

    def step(at):
        unit, _inv = standardize(frames_ref[at, :].astype(F32))
        normed = (unit * whole_ref[0:1, :] + whole_ref[2:3, :]).astype(BF)
        normed_ref[at, :] = normed
        normedT_ref[:, at] = normed.T
        sum_ref[...] += jnp.sum(cot_ref[at, :].astype(F32), axis=0, keepdims=True)

    blocks(frames_ref.shape[0], step)


def enter(pos, frames, cot, small, far):
    rows, width = frames.shape
    group = width // GROUPS
    outs = (array((rows, width)), array((width, rows)), array((1, width), F32), array((8, width), F32))
    return call(
        functools.partial(enter_kernel, group), "enter", outs + (array((1, 3 * group), F32),) * GROUPS, 5, 1,
        flops=rows * width * 20, moved=rows * width * 8, far=(1,),
    )(pos, frames, cot, small, far)


def pack_kernel(group, done, need, pos_ref, w_ref, *outs):
    half = w_ref.shape[0] // 2
    d = group * GROUPS
    at = pl.ds(pl.multiple_of(pos_ref[1] * half, half), half)
    for g in range(GROUPS):
        for t in range(3):
            cols = slice(t * d + g * group, t * d + (g + 1) * group)
            to = slice(t * group, (t + 1) * group)
            outs[g][:, to] = w_ref[at, cols]
            outs[GROUPS + g][:, to] = w_ref[:, cols]


def pack(pos, w):
    rows, cols = w.shape
    group = cols // 3 // GROUPS
    return call(
        functools.partial(pack_kernel, group), "pack",
        (array((rows // 2, 3 * group)),) * GROUPS + (array((rows, 3 * group)),) * GROUPS, 2, 1, moved=rows * cols * 5,
    )(pos, w)


def pack_more_kernel(done, need, pos_ref, out_ref, up_ref, down_ref, half_ref, *outs):
    core = pos_ref[1]
    half = half_ref.shape[0]
    half_ref[...] = out_ref[pl.ds(pl.multiple_of(core * half, half), half), :]
    chunks = len(outs) // 2
    up_rows, down_rows = up_ref.shape[0] // 2, down_ref.shape[0] // chunks // 2
    chunk = 2 * down_rows
    for i in range(chunks):
        at = pl.ds(pl.multiple_of(core * up_rows, up_rows), up_rows)
        outs[2 * i][...] = up_ref[at, i * chunk : (i + 1) * chunk]
        at = pl.ds(pl.multiple_of(i * chunk + core * down_rows, down_rows), down_rows)
        outs[2 * i + 1][...] = down_ref[at, :]


def pack_more(pos, w_out, w_up, w_down, chunks):
    d, hid = w_up.shape
    chunk = hid // chunks
    return call(
        pack_more_kernel, "pack_more",
        (array((w_out.shape[0] // 2, d)),) + (array((d // 2, chunk)), array((chunk // 2, d))) * chunks, 4, 1,
        moved=d * hid * 6,
    )(pos, w_out, w_up, w_down)


def windows(seg):
    length = seg.shape[1]
    first = seg[0, ::BLK]
    last = seg[0, BLK - 1 :: BLK]
    begin = jnp.sum((seg < first[:, None]).astype(jnp.int32), axis=1)
    end = jnp.sum((seg <= last[:, None]).astype(jnp.int32), axis=1)
    begin = begin // 16 * 16
    count = (end - begin + BLK - 1) // BLK
    begin = jnp.minimum(begin, length - count * BLK)
    return jnp.stack([begin, count]).astype(jnp.int32)


def by_head(block, dh):
    width = block.shape[1]
    lane = lax.broadcasted_iota(jnp.int32, (1, width), 1) // dh
    zero = jnp.zeros_like(block)
    return jnp.concatenate([jnp.where(lane == h, block, zero) for h in range(width // dh)], axis=0)


def place(full_ref, pos_ref, own_ref, near_ref, far_ref):
    shard, core = pos_ref[0], pos_ref[1]
    size = own_ref.shape[0]
    half = size // 2
    full_ref[pl.ds(pl.multiple_of(shard * size, half), size), :] = own_ref[...]
    for k in range(near_ref.shape[0]):
        base = jnp.bitwise_xor(shard, k + 1) * size
        full_ref[pl.ds(pl.multiple_of(base + core * half, half), half), :] = near_ref[k]
        full_ref[pl.ds(pl.multiple_of(base + (1 - core) * half, half), half), :] = far_ref[k]


def attn_fwd_kernel(dh, done, need, pos_ref, win_ref, normed_ref, own_ref, near_ref, far_ref, bias_ref, segr_ref, segc_ref,
                    w_ref, proj_ref, att_ref, attT_ref, lse_ref, acc_ref):
    width = att_ref.shape[1]
    heads = width // dh
    length = normed_ref.shape[0]
    place(w_ref, pos_ref, own_ref, near_ref, far_ref)

    def project(i, _):
        at = rows_of(i)
        proj_ref[at, :] = (mm(normed_ref[at, :], w_ref[...]) + bias_ref[...]).astype(BF)
        return 0

    lax.fori_loop(0, length // BLK, project, 0)
    done(0)
    done(1)

    def queries(step, _):
        at = rows_of(step)
        q = (proj_ref[at, 0:width].astype(F32) * (1.0 / math.sqrt(dh))).astype(BF)
        qall = by_head(q, dh)
        segq = jnp.concatenate([segr_ref[:, at]] * heads, axis=1)
        acc_ref[...] = jnp.zeros_like(acc_ref)
        start = win_ref[0, step]

        def tile(j, carry):
            m_old, mass = carry
            ks = pl.ds(pl.multiple_of(start + j * BLK, 16), BLK)
            vT = proj_ref[ks, 2 * width : 3 * width].T
            same = segc_ref[ks, :] == segq
            s = jnp.where(same, mm(proj_ref[ks, width : 2 * width], qall, NT), NEG)
            m_new = jnp.maximum(m_old, jnp.max(s, axis=0, keepdims=True))
            p = jnp.exp(s - m_new)
            alpha = jnp.exp(m_old - m_new)
            mass = mass * alpha + jnp.sum(p, axis=0, keepdims=True)
            pb = p.astype(BF)
            for h in range(heads):
                hs, cs = slice(h * dh, (h + 1) * dh), slice(h * BLK, (h + 1) * BLK)
                acc_ref[hs, :] = acc_ref[hs, :] * alpha[:, cs] + mm(vT[hs, :], pb[:, cs])
            return m_new, mass

        carry = (jnp.full((1, heads * BLK), NEG, F32), jnp.zeros((1, heads * BLK), F32))
        peak, mass = lax.fori_loop(0, win_ref[1, step], tile, carry)
        lse_ref[:, rows_of(step, heads * BLK)] = peak + jnp.log(mass)
        outs = []
        for h in range(heads):
            outs.append((acc_ref[h * dh : (h + 1) * dh, :] / mass[:, h * BLK : (h + 1) * BLK]).astype(BF))
        oT = jnp.concatenate(outs, axis=0)
        attT_ref[:, at] = oT
        att_ref[at, :] = oT.T
        return 0

    lax.fori_loop(0, length // BLK, queries, 0)


def attn_fwd(dh, pos, win, normed, own, near, far, bias, segr, segc):
    length, d = normed.shape
    width = own.shape[1] // 3
    heads = width // dh
    return call(
        functools.partial(attn_fwd_kernel, dh), "attn_fwd",
        (array((d, 3 * width)), array((length, 3 * width)), array((length, width)), array((width, length)),
         array((1, length * heads), F32)),
        9, 2, [pltpu.VMEM((width, BLK), F32)],
        flops=2 * length * d * 3 * width + 2 * length * length * 256 * heads,
        moved=length * (d + 6 * width) * 2, far=(0, 1, 3), cost=0.1,
    )(pos, win, normed, own, near, far, bias, segr, segc)


def split_rows(pos_ref, left_ref, right, keep_ref, send_ref, first):
    shard, core = pos_ref[0], pos_ref[1]
    half = left_ref.shape[0] // keep_ref.shape[0] // 2
    for k in range(keep_ref.shape[0]):
        base = jnp.bitwise_xor(shard, k) * (2 * half)
        for ref, part in ((keep_ref, core), (send_ref, 1 - core)):
            rs = pl.ds(pl.multiple_of(base + part * half, half), half)
            ref[k, first : first + half, :] = mm(left_ref[rs, :], right).astype(BF)


def attn_bwd_kernel(dh, extra, done, need, pos_ref, win_ref, proj_ref, att_ref, g_ref, lse_ref, segr_ref, segc_ref, nT_ref, *refs):
    if extra:
        more_keep_ref, more_send_ref = refs[:2]
        refs = refs[2:]
    dproj_ref, keep_ref, send_ref, sums_ref, dk_ref, dv_ref, dqT_ref = refs
    length, width = att_ref.shape
    heads = width // dh
    scale = 1.0 / math.sqrt(dh)
    dk_ref[...] = jnp.zeros_like(dk_ref)
    dv_ref[...] = jnp.zeros_like(dv_ref)
    row = lax.broadcasted_iota(jnp.int32, (8, width), 0)
    col = lax.broadcasted_iota(jnp.int32, (8, width), 1) // dh
    pick = jnp.where(row == col, 1.0, 0.0).astype(BF)

    def queries(step, _):
        at = rows_of(step)
        q = (proj_ref[at, 0:width].astype(F32) * scale).astype(BF)
        g = g_ref[at, :]
        qall = by_head(q, dh)
        gall = by_head(g, dh)
        og = att_ref[at, :].astype(F32) * g.astype(F32)
        high = og.astype(BF)
        low = (og - high.astype(F32)).astype(BF)
        delta = mm(pick, high, NT) + mm(pick, low, NT)
        delta = jnp.concatenate([delta[h : h + 1, :] for h in range(heads)], axis=1)
        lse = lse_ref[:, rows_of(step, heads * BLK)]
        segq = jnp.concatenate([segr_ref[:, at]] * heads, axis=1)
        dqT_ref[...] = jnp.zeros_like(dqT_ref)
        start = win_ref[0, step]

        def tile(j, _):
            ks = pl.ds(pl.multiple_of(start + j * BLK, 16), BLK)
            kt = proj_ref[ks, width : 2 * width]
            vt = proj_ref[ks, 2 * width : 3 * width]
            kT = kt.T
            same = segc_ref[ks, :] == segq
            p = jnp.where(same, jnp.exp(mm(kt, qall, NT) - lse), 0.0)
            ds = (p * (mm(vt, gall, NT) - delta)).astype(BF)
            dv_ref[ks, :] += mm(p.astype(BF), gall)
            dk_ref[ks, :] += mm(ds, qall)
            for h in range(heads):
                hs = slice(h * dh, (h + 1) * dh)
                dqT_ref[hs, :] += mm(kT[hs, :], ds[:, h * BLK : (h + 1) * BLK])
            return 0

        lax.fori_loop(0, win_ref[1, step], tile, 0)
        dproj_ref[at, 0:width] = (dqT_ref[...] * scale).astype(BF).T
        return 0

    lax.fori_loop(0, length // BLK, queries, 0)
    dproj_ref[:, width : 2 * width] = dk_ref[...].astype(BF)
    dproj_ref[:, 2 * width :] = dv_ref[...].astype(BF)
    sums_ref[...] = jnp.sum(dproj_ref[...].astype(F32), axis=0, keepdims=True)
    first = 0
    if extra:
        first = more_keep_ref.shape[1]
        keep_ref[:, 0:first, :] = more_keep_ref[...]
        send_ref[:, 0:first, :] = more_send_ref[...]
    done(0)
    split_rows(pos_ref, nT_ref, dproj_ref[...], keep_ref, send_ref, first)


def attn_bwd(dh, pos, win, shards, proj, att, g, lse, segr, segc, nT, extra=()):
    length, width = att.shape
    d = nT.shape[0]
    heads = width // dh
    half = d // shards // 2 + (extra[0].shape[1] if extra else 0)
    return call(
        functools.partial(attn_bwd_kernel, dh, bool(extra)), "attn_bwd",
        (array((length, 3 * width)), array((shards, half, 3 * width)), array((shards, half, 3 * width)), array((1, 3 * width), F32)),
        9 + len(extra), 2, [pltpu.VMEM((length, width), F32), pltpu.VMEM((length, width), F32), pltpu.VMEM((width, BLK), F32)],
        flops=2 * length * d * 3 * width + 5 * length * length * 256 * heads,
        moved=length * (d + 8 * width) * 2, far=(0,),
    )(pos, win, proj, att, g, lse, segr, segc, nT, *extra)


def middle_kernel(done, need, pos_ref, frames_ref, a0, a1, a2, own_ref, near_ref, far_ref, whole_ref,
                  w_ref, middle_ref, n_ref, nT_ref):
    place(w_ref, pos_ref, own_ref, near_ref, far_ref)
    width = a0.shape[1]

    def step(at):
        total = frames_ref[at, :].astype(F32) + whole_ref[6:7, :]
        for g, a in enumerate((a0, a1, a2)):
            total = total + mm(a[at, :], w_ref[g * width : (g + 1) * width, :])
        middle_ref[at, :] = total
        unit, _inv = standardize(total)
        normed = (unit * whole_ref[1:2, :] + whole_ref[3:4, :]).astype(BF)
        n_ref[at, :] = normed
        nT_ref[:, at] = normed.T

    blocks(frames_ref.shape[0], step)


def middle(pos, frames, atts, own, near, far, whole):
    rows, d = frames.shape
    return call(
        middle_kernel, "middle",
        (array((d, d)), array((rows, d), F32), array((rows, d)), array((d, rows))), 9, 1,
        flops=2 * rows * d * d, moved=rows * d * 12, far=(0, 1), cost=0.1,
    )(pos, frames, *atts, own, near, far, whole)


def ffn_kernel(own, apart, fresh, offset, done, need, pos_ref, n_ref, nT_ref, cot_ref, *refs):
    refs = list(refs)
    first, second = refs.pop(0), refs.pop(0)
    if apart:
        first, second = (first, second), (refs.pop(0), refs.pop(0))
    bias_ref = refs.pop(0)
    prev_ref = None if fresh else refs.pop(0)
    act_ref, keep_ref, send_ref, bsum_ref, gn_ref = refs[:5]
    core = pos_ref[1]
    if own:
        up_ref, down_ref = first, second
    else:
        down_ref, up_ref = refs[5], refs[6]
        for ref, t in ((up_ref, 0), (down_ref, 1)):
            size = ref.shape[0] // 2
            ref[pl.ds(pl.multiple_of(core * size, size), size), :] = first[t][...]
            ref[pl.ds(pl.multiple_of((1 - core) * size, size), size), :] = second[t][...]
    d = n_ref.shape[1]
    chunk = act_ref.shape[1]

    if not own:
        done(5)
    up = up_ref[:, offset : offset + chunk]
    down = down_ref[offset : offset + chunk, :]
    acts, ghs = [], []
    for i in range(n_ref.shape[0] // BLK):
        at = slice(i * BLK, (i + 1) * BLK)
        hidden = mm(n_ref[at, :], up) + bias_ref[...]
        grad = mm(cot_ref[at, :], down, NT)
        phi = 0.5 + 0.5 * lax.erf(hidden * (1.0 / math.sqrt(2.0)))
        bell = jnp.exp(hidden * hidden * -0.5) * (1.0 / math.sqrt(2.0 * math.pi))
        act = (hidden * phi).astype(BF)
        gh = (grad * (phi + hidden * bell)).astype(BF)
        act_ref[at, :] = act
        base = jnp.zeros((BLK, d), F32) if fresh else prev_ref[at, :]
        gn_ref[at, :] = base + mm(gh, up, NT)
        acts.append(act)
        ghs.append(gh)
    done(0)
    act = jnp.concatenate(acts, axis=0)
    gh = jnp.concatenate(ghs, axis=0)
    bsum_ref[...] = jnp.sum(gh.astype(F32), axis=0, keepdims=True)
    d_down = mm(act, cot_ref[...], TN).astype(BF)
    d_up = mm(nT_ref[...], gh).astype(BF)
    if d > chunk:
        d_up = jnp.concatenate([d_up[r * chunk : (r + 1) * chunk, :] for r in range(d // chunk)], axis=1)
    first = core == 0
    keep_ref[...] = jnp.where(first, d_down, d_up)
    send_ref[...] = jnp.where(first, d_up, d_down)


def ffn(own, offset, pos, n, nT, cot, first, second, bias, grad):
    rows, d = n.shape
    chunk = bias.shape[1]
    fresh = grad is None
    apart = isinstance(first, tuple)
    args = [pos, n, nT, cot, *(first + second if apart else (first, second)), bias] + ([] if fresh else [grad])
    outs = (array((rows, chunk)), array((chunk, d)), array((chunk, d)), array((1, chunk), F32), array((rows, d), F32))
    if not own:
        outs = outs + (array((chunk, d)),)
    return call(
        functools.partial(ffn_kernel, own, apart, fresh, offset), "ffn", outs,
        len(args), 1, [] if own else [pltpu.VMEM((d, chunk), BF)], flops=10 * rows * d * chunk,
        moved=rows * d * 20,
        far=(0,) if own else (0, 5), limit=20 << 20,
    )(*args)


def turn_kernel(done, need, pos_ref, gn_ref, middle_ref, cot_ref, whole_ref, w_ref, t0, t1, t2,
                gm_ref, g0, g1, g2, keep_ref, send_ref, sums_ref, branch_ref, mixT_ref):
    width = g0.shape[1]
    sums_ref[...] = jnp.zeros_like(sums_ref)
    for g, t in enumerate((t0, t1, t2)):
        mixT_ref[g * width : (g + 1) * width, :] = t[...]

    def step(at):
        gn = gn_ref[at, :]
        unit, inverse = standardize(middle_ref[at, :])
        e = gn * whole_ref[1:2, :]
        gm = cot_ref[at, :].astype(F32) + inverse * (
            e - jnp.mean(e, axis=1, keepdims=True) - unit * jnp.mean(e * unit, axis=1, keepdims=True)
        )
        gm_ref[at, :] = gm
        branch = gm.astype(BF)
        branch_ref[at, :] = branch
        sums_ref[0:1, :] += jnp.sum(gn * unit, axis=0, keepdims=True)
        sums_ref[1:2, :] += jnp.sum(gn, axis=0, keepdims=True)
        sums_ref[2:3, :] += jnp.sum(branch.astype(F32), axis=0, keepdims=True)
        for g, out in enumerate((g0, g1, g2)):
            out[at, :] = mm(branch, w_ref[g * width : (g + 1) * width, :], NT).astype(BF)

    blocks(gn_ref.shape[0], step)
    split_rows(pos_ref, mixT_ref, branch_ref[...], keep_ref, send_ref, 0)


def turn(pos, shards, gn, mid, cot, whole, w, attTs):
    rows, d = gn.shape
    width = d // GROUPS
    return call(
        turn_kernel, "turn",
        (array((rows, d), F32),) + (array((rows, width)),) * 3 + (array((shards, d // shards // 2, d)),) * 2 + (array((8, d), F32),),
        9, 1, [pltpu.VMEM((rows, d), BF), pltpu.VMEM((d, rows), BF)],
        flops=4 * rows * d * d, moved=rows * d * 20,
    )(pos, gn, mid, cot, whole, w, *attTs)


def leave_kernel(shards, ups, done, need, pos_ref, frames_ref, gm_ref, whole_ref, p0, p1, p2, w0, w1, w2, two_ref, cot_ref, *refs):
    qv_refs, up_refs, (out_ref, small_ref, tall_ref) = refs[:GROUPS], refs[GROUPS : GROUPS + ups], refs[GROUPS + ups :]
    tall_ref[...] = jnp.zeros_like(tall_ref)

    def step(at):
        gn = 0.0
        for i, (p, w) in enumerate(((p0, w0), (p1, w1), (p2, w2))):
            need(4 + i)
            need(7 + i)
            gn = gn + mm(p[at, :], w[...], NT)
        unit, inverse = standardize(frames_ref[at, :].astype(F32))
        e = gn * whole_ref[0:1, :]
        out_ref[at, :] = gm_ref[at, :] + inverse * (
            e - jnp.mean(e, axis=1, keepdims=True) - unit * jnp.mean(e * unit, axis=1, keepdims=True)
        )
        tall_ref[0:1, :] += jnp.sum(gn * unit, axis=0, keepdims=True)
        tall_ref[2:3, :] += jnp.sum(gn, axis=0, keepdims=True)

    blocks(frames_ref.shape[0], step)
    tall_ref[1:2, :] = two_ref[0:1, :]
    tall_ref[3:4, :] = two_ref[1:2, :]
    tall_ref[6:7, :] = two_ref[2:3, :]
    tall_ref[7:8, :] = cot_ref[...]
    for g, ref in enumerate(qv_refs):
        width = ref.shape[1] // 3
        cols = slice(g * width, (g + 1) * width)
        tall_ref[4:5, cols] = ref[:, 0:width]
        tall_ref[5:6, cols] = ref[:, 2 * width :]
    size = tall_ref.shape[1] // shards
    for k in range(shards):
        want = jnp.bitwise_xor(pos_ref[0], k)
        value = jnp.zeros((8, size), F32)
        for j in range(shards):
            value = jnp.where(want == j, tall_ref[:, j * size : (j + 1) * size], value)
        small_ref[k, 0:8, :] = value
        row = 8
        for ref in up_refs[k * ups // shards : (k + 1) * ups // shards]:
            for c in range(ref.shape[1] // size):
                small_ref[k, row : row + 1, :] = ref[:, c * size : (c + 1) * size]
                row += 1


def leave(pos, shards, frames, gm, whole, dprojs, ws, two, cot_sum, qvs, ups):
    rows, d = frames.shape
    return call(
        functools.partial(leave_kernel, shards, len(ups)), "leave",
        (array((rows, d), F32), array((shards, 12, d // shards), F32)), 12 + len(qvs) + len(ups), 1,
        [pltpu.VMEM((8, d), F32)], flops=6 * rows * d * d, moved=rows * d * 16, far=(0,),
        fetch={4 + i: array(v.shape) for i, v in enumerate((*dprojs, *ws))}, limit=30 << 20,
    )(pos, frames, gm, whole, *dprojs, *ws, two, cot_sum, *qvs, *ups)


def result_kernel(n, offsets, done, need, middle_ref, whole_ref, *refs):
    acts, downs, out_ref = refs[:n], refs[n : 2 * n], refs[2 * n]
    need(0)

    def step(at):
        total = middle_ref[at, :] + whole_ref[7:8, :]
        for i, (a, w, offset) in enumerate(zip(acts, downs, offsets)):
            need(2 + i)
            need(2 + n + i)
            total = total + mm(a[at, :], w[offset : offset + a.shape[1], :])
        out_ref[at, :] = total.astype(BF)

    blocks(middle_ref.shape[0], step)


def result(mid, whole, acts, downs, offsets):
    rows, d = mid.shape
    n = len(acts)
    fetch = {0: array(mid.shape, F32)}
    fetch.update({2 + i: array(v.shape) for i, v in enumerate((*acts, *downs))})
    return call(
        functools.partial(result_kernel, n, offsets), "result", array((rows, d)), 2 + 2 * n, 0,
        flops=2 * rows * d * n * acts[0].shape[1], moved=rows * d * 14, far=(0,), fetch=fetch, limit=36 << 20,
    )(mid, whole, *acts, *downs)


def swap(value, axis, size, bit):
    return lax.ppermute(value, axis, [(i, i ^ bit) for i in range(size)])


def after(value, *others):
    return lax.optimization_barrier((value, *others))[0]


def total(terms):
    out = terms[0].astype(F32)
    for t in terms[1:]:
        out = out + t.astype(F32)
    return out.astype(terms[0].dtype)


def bits_of(size):
    return [1 << b for b in range(size.bit_length() - 1)]


def spread(own, shards):
    stack = own[None]
    for bit in bits_of(shards):
        stack = jnp.concatenate([stack, swap(stack, "shard", shards, bit)], axis=0)
    return stack


def others(own, shards):
    return swap(own, "shard", 2, 1)[None] if shards == 2 else spread(own, shards)[1:]


class Order:
    def __init__(self):
        self.token = None
        self.pins = []

    def land(self, *values):
        if self.token is not None:
            values = lax.optimization_barrier((*values, self.token))[:-1]
        self.pins += values
        return values[0] if len(values) == 1 else values

    def hold(self, *values):
        self.pins += values
        return values[0] if len(values) == 1 else values

    def run(self, kernel, value, token):
        if self.pins or self.token is not None:
            value = after(value, *self.pins, *([] if self.token is None else [self.token]))
        self.pins = []
        out = kernel(value)
        self.token = out[token]
        return out


def combine_kernel(groups, done, need, flag_ref, *refs):
    outs = list(refs[sum(len(terms) for terms, _ in groups) :])
    at = 0
    for terms, cut in groups:
        ins = refs[at : at + len(terms)]
        at += len(terms)

        def summed(rs):
            out = 0.0
            for ref, lead in zip(ins, terms):
                out = out + (ref[rs, :] if lead is None else ref[lead, rs, :]).astype(F32)
            return out

        if cut:
            send, keep = outs.pop(0), outs.pop(0)
            rows = send.shape[0]
            for ref, half in ((send, 1 - flag_ref[0]), (keep, flag_ref[0])):
                ref[...] = summed(pl.ds(pl.multiple_of(half * rows, rows), rows)).astype(ref.dtype)
        else:
            out = outs.pop(0)
            out[...] = summed(slice(None)).astype(out.dtype)


def combine(flag, groups):
    terms, spec, outs = [], [], []
    for group, cut in groups:
        group = [t if isinstance(t, tuple) else (t, None) for t in group]
        terms += [t for t, _ in group]
        spec.append(([lead for _, lead in group], cut))
        rows, cols = group[0][0].shape[-2:]
        outs += [array((rows // 2, cols), group[0][0].dtype)] * 2 if cut else [array((rows, cols), group[0][0].dtype)]
    return call(
        functools.partial(combine_kernel, spec), "combine", tuple(outs), 1 + len(terms), 1, flops=1000, limit=6 << 20,
    )(flag, *terms)


def join_kernel(done, need, flag_ref, part_ref, other_ref, out_ref):
    rows = part_ref.shape[0]
    for ref, half in ((part_ref, flag_ref[0]), (other_ref, 1 - flag_ref[0])):
        out_ref[pl.ds(pl.multiple_of(half * rows, rows), rows), :] = ref[...]


def join(flag, part, other):
    rows, cols = part.shape
    return call(join_kernel, "join", array((2 * rows, cols), part.dtype), 3, 1, flops=1000, limit=6 << 20)(flag, part, other)[0]


class Ring:
    def __init__(self, shards, replicas, order):
        self.shards, self.replicas, self.order = shards, replicas, order
        self.bits = bits_of(replicas)[1:]
        replica = lax.axis_index("replica")
        self.flags = {bit: ((replica // bit) % 2).astype(jnp.int32)[None] for bit in bits_of(replicas)}

    def swap(self, value, bit):
        return swap(value, "replica", self.replicas, bit)

    def total(self, terms):
        return combine(self.flags[1], [(terms, False)])[0] if len(terms) > 1 else terms[0]

    def to_shard(self, pieces):
        for bit in reversed(bits_of(self.shards)):
            if bit == 1:
                send = self.order.hold(self.total(pieces[1]))
                return pieces[0], swap(send, "shard", self.shards, bit)
            send = self.order.hold(jnp.stack([self.total(p) for p in pieces[bit:]]))
            got = swap(send, "shard", self.shards, bit)
            pieces = [p + [(got, k)] for k, p in enumerate(pieces[:bit])]

    def to_halves(self, chunks, bit):
        outs = combine(self.flags[bit], [(terms, True) for terms in chunks])
        self.order.hold(*outs)
        return [([outs[2 * i + 1]], self.swap(outs[2 * i], bit)) for i in range(len(chunks))]

    def to_half(self, terms, bit):
        return self.to_halves([terms], bit)[0]

    def whole(self, part, bit):
        return join(self.flags[bit], part, self.swap(part, bit))

    def both(self, part, bit):
        return self.total([part, self.swap(part, bit)])


def local(replicas, shards, frames, cotangent, segment_ids, norm_gain, norm_bias, w_qkv, qv_bias, w_out, out_bias,
          w_up, up_bias, w_down):
    rows, d = frames.shape
    dh = d // H
    group = d // GROUPS
    hid = up_bias.shape[0]
    chunks = max(1, hid // d)
    chunk = hid // chunks
    shard = lax.axis_index("shard")
    core = lax.axis_index("replica") % 2
    pos = jnp.stack([shard, core]).astype(jnp.int32)
    order = Order()
    ring = Ring(shards, replicas, order)
    run, land, hold = order.run, order.land, order.hold
    twin = lambda v: ring.swap(v, 1)
    win = windows(segment_ids)
    segc = segment_ids.reshape(rows, 1)
    bias_own = up_bias.reshape(1, hid)

    small = jnp.concatenate([norm_gain, norm_bias, qv_bias, out_bias], axis=0)
    small_far = others(small, shards)
    packed = run(lambda v: pack(pos, v), w_qkv, 0)
    qkv_own = packed[GROUPS:]
    near = [others(packed[0], shards)]
    bias_far = others(bias_own, shards)
    more = run(lambda v: pack_more(pos, v, w_up, w_down, chunks), w_out, 0)
    pairs = [(more[1 + 2 * i], more[2 + 2 * i]) for i in range(chunks)]
    if chunk == d:
        pairs = [(jnp.stack(p),) for p in pairs]
    small_far = land(small_far)
    bias_far = land(bias_far)
    normed, normedT, cot_sum, whole, *qv = run(lambda v: enter(pos, v, cotangent, small, small_far), frames, 2)
    near[0] = land(near[0])
    far = [land(twin(near[0]))]
    near += [others(after(packed[g], near[0]), shards) for g in range(1, GROUPS)]

    ws, projs, atts, attTs, lses = [], [], [], [], []
    for g in range(GROUPS):
        w, proj, att, attT, lse = run(
            lambda v: attn_fwd(dh, pos, win, v, qkv_own[g], near[g], far[g], qv[g], segment_ids, segc), normed, 4)
        ws.append(w)
        projs.append(proj)
        atts.append(att)
        attTs.append(attT)
        lses.append(lse)
        if g == 0:
            near[1:] = land(*near[1:])
            far += land(*[twin(v) for v in near[1:]])
            near_out = others(after(more[0], near[1]), shards)
            fetched = [[others(after(v, *far[1:]), shards) for v in pairs[0]]]
        if g == 1:
            fetched += [[others(after(v, lse), shards) for v in pairs[i]] for i in range(1, chunks)]
    near_out = land(near_out)
    far_out = land(twin(near_out))
    w_out_all, mid, n_two, nT_two = run(lambda v: middle(pos, v, atts, w_out, near_out, far_out, whole), frames, 3)

    grad, acts, downs, offsets, up_sums = None, [], [], [], []
    pieces = [[None] * shards for _ in range(chunks)]
    waiting, pending = [], []
    chains, got = [None] * chunks, [None] * chunks
    x = ring.bits[0]
    brought = [None] * chunks
    for k in range(shards):
        for i in range(chunks):
            bias = (bias_own if k == 0 else bias_far[k - 1])[:, i * chunk : (i + 1) * chunk].astype(F32)
            if k == 0:
                out = run(lambda v: ffn(True, i * chunk, pos, v, nT_two, cotangent, w_up, w_down, bias, grad), n_two, 3)
                downs.append(w_down)
                offsets.append(i * chunk)
            else:
                if brought[i] is None:
                    a = [land(v) for v in fetched[i]]
                    brought[i] = a, [land(twin(v)) for v in a]
                elif late[0] is not None:
                    brought[0] = brought[0][0], [land(v) for v in late[0]]
                    late[0] = None
                a, b = [tuple(v[k - 1] for v in half) for half in brought[i]]
                a, b = (a[0], b[0]) if len(a) == 1 else (a, b)
                out = run(lambda v: ffn(False, 0, pos, v, nT_two, cotangent, a, b, bias, grad), n_two, 3)
                downs.append(out[5])
                offsets.append(0)
            if k == 0 and i == 0:
                a = [land(v) for v in fetched[0]]
                late = [[twin(v) for v in a]]
                brought[0] = a, None
            acts.append(out[0])
            up_sums.append(out[3])
            grad = out[4]
            last = k == shards - 1
            if k == 0 and shards == 2:
                pieces[i][k] = [out[1]]
                waiting.append((i, out[2]))
            elif last and i == chunks - 1 and i % 2:
                pieces[i][k] = [out[1]]
                final = twin(hold(out[2]))
                for j, other in pending:
                    pieces[j][0].append(land(other))
                pending = []
                continue
            else:
                pieces[i][k] = [out[1], land(twin(out[2]))]
                early = [(j, twin(after(send, pieces[i][k][1]))) for j, send in waiting]
                for j, other in pending:
                    pieces[j][0].append(land(other))
                waiting, pending = [], early
            if last:
                if i % 2 == 0:
                    chains[i], got[i] = ring.to_shard(pieces[i])
                else:
                    chains[i] = ring.to_halves(pieces[i], x)

    out = run(lambda v: turn(pos, shards, v, mid, cotangent, whole, w_out_all, attTs), grad, 6)
    gm, gs, out_keep, out_send, sums_two = out[0], out[1:4], out[4], out[5], out[6]
    if chunks % 2 == 0:
        pieces[-1][-1].append(land(final))
        chains[-1] = ring.to_halves(pieces[-1], x)
    dprojs, qv_sums, attn = [], [], []

    def back(g, extra=(), go=True):
        dproj, keep, send, sums = run(
            lambda v: attn_bwd(dh, pos, win, shards, projs[g], atts[g], v, lses[g], segment_ids, segc, normedT, extra), gs[g], 3)
        dprojs.append(dproj)
        qv_sums.append(sums)
        return keep, twin(hold(send)) if go else send

    def meet(keep, other):
        other = land(other)
        return ring.to_shard([[(keep, k), (other, k)] for k in range(shards)])

    z, far_bit, *last_bits = ring.bits[1:]
    even, odd = range(0, chunks, 2), range(1, chunks, 2)
    one = back(0, (out_keep, out_send))
    for i in even:
        chains[i], got[i] = ring.to_half(chains[i] + [land(got[i])], x)
    keep, send = back(1, (), False)
    for i in odd:
        chains[i], got[i] = ring.to_shard([keep_ + [land(v)] for keep_, v in chains[i]])
    one, one_got = meet(*one)
    two = back(2, (keep, send))
    for i in (*even, *odd):
        chains[i], got[i] = ring.to_half(chains[i] + [land(got[i])], z)
    d_frames, small_grads = run(
        lambda v: leave(pos, shards, frames, v, whole, dprojs, ws, sums_two, cot_sum, qv_sums, up_sums), gm, 1)
    two, two_got = meet(*two)
    one, one_got = ring.to_half(one + [land(one_got)], x)
    for i in range(chunks):
        chains[i] = hold(ring.total(chains[i] + [land(got[i])]))
        got[i] = ring.swap(chains[i], far_bit)
        order.token = chains[i]
    small, small_got = ring.to_shard([[small_grads[k]] for k in range(shards)])
    small = hold(ring.total(small + [land(small_got)]))
    small_got = ring.swap(small, x)
    out_frames, = run(lambda v: result(v, whole, acts, downs, tuple(offsets)), mid, 0)

    def add_step(part, other):
        order.token = ring.total([*part, after(other, order.token)])
        return order.token

    def join_step(part, other, bit):
        order.token = join(ring.flags[bit], part, after(other, order.token))
        return order.token

    full, wait = [None] * chunks, [None] * chunks

    def add_far(i):
        full[i] = add_step([chains[i]], got[i])
        for bit in last_bits:
            full[i] = add_step([full[i]], ring.swap(full[i], bit))
        wait[i] = ring.swap(full[i], z)

    def join_next(i, bit, next_bit):
        full[i] = join_step(full[i], wait[i], bit)
        wait[i] = ring.swap(full[i], next_bit)

    tail = range(1, chunks)
    small = add_step([small], small_got)
    small_got = ring.swap(small, z)
    add_far(0)
    one = add_step(one, one_got)
    one_got = ring.swap(one, z)
    send, keep = combine(ring.flags[x], [([*two, after(two_got, order.token)], True)])
    order.token = send
    two_got = ring.swap(send, x)
    for i in tail:
        add_far(i)
    join_next(0, z, x)
    two = add_step([keep], two_got)
    two_got = ring.swap(two, z)
    one = add_step([one], one_got)
    one_got = ring.swap(one, far_bit)
    small = add_step([small], small_got)
    small_got = ring.swap(small, 1)
    small = add_step([small], small_got)
    small_got = ring.swap(small, far_bit)
    for i in tail:
        join_next(i, z, x)
    two = add_step([two], two_got)
    two_got = ring.swap(two, far_bit)
    join_next(0, x, 1)
    one = add_step([one], one_got)
    small = add_step([small], small_got)
    for bit in last_bits:
        one = add_step([one], ring.swap(one, bit))
        small = add_step([small], ring.swap(small, bit))
    one_got = ring.swap(one, x)
    two = add_step([two], two_got)
    for bit in last_bits:
        two = add_step([two], ring.swap(two, bit))
    two_got = ring.swap(two, x)
    for i in tail:
        join_next(i, x, 1)
    one = join_step(one, one_got, x)
    two = join_step(two, two_got, x)
    vec = small
    ffn_grads = [
        (jnp.where(core == 0, mine, other), jnp.where(core == 0, other, mine)) for mine, other in zip(full, wait)]
    attn_grads = []
    for mine in (one, two):
        other = twin(mine)
        attn_grads.append((jnp.where(core == 0, mine, other), jnp.where(core == 0, other, mine)))

    d_down = jnp.concatenate([c[0] for c in ffn_grads], axis=0).astype(F32)
    ups = []
    for c in ffn_grads:
        up = c[1]
        ups.append(jnp.concatenate([up[:, r * chunk : (r + 1) * chunk] for r in range(d // chunk)], axis=0))
    d_up = jnp.concatenate(ups, axis=1).astype(F32)
    half = d // shards // 2
    d_wout = jnp.concatenate([v[:half] for v in attn_grads[0]]).astype(F32)
    groups = [[v[half:] for v in attn_grads[0]], [v[:half] for v in attn_grads[1]], [v[half:] for v in attn_grads[1]]]
    d_qkv = jnp.concatenate([
        jnp.concatenate([g[c][:, t * group : (t + 1) * group] for t in range(3) for g in groups], axis=1)
        for c in range(2)]).astype(F32)
    return (
        out_frames, d_frames, vec[0:2], vec[2:4], d_qkv, vec[4:6], d_wout, vec[6:8], d_up,
        vec[8:].reshape(hid), d_down,
    )


def solution(mesh):
    both = P(("replica", "shard"), None)
    wide, tall, flat = P(None, "shard"), P("shard", None), P("shard")
    return jax.shard_map(
        functools.partial(local, mesh.shape["replica"], mesh.shape["shard"]),
        mesh=mesh,
        in_specs=(both, both, both, wide, wide, tall, wide, tall, wide, wide, flat, tall),
        out_specs=(both, both, wide, wide, tall, wide, tall, wide, wide, flat, tall),
        check_vma=False,
    )
```
